32 devices in a mesh: tm: 16 (over z, y, core), grp: 2 (over x).
Axes of the slice: x: 2, y: 2, z: 4, core: 2. Of those that a mesh axis runs over, the one named last changes fastest.
Arguments:
- features: bfloat16 [4096, 512], P(('tm', 'grp')), may hold values from -6 to 6
- weight_five: bfloat16 [2, 512, 512], P(None, None, 'tm'), may hold values from -0.1875 to 0.1875
- weight_six: bfloat16 [2, 512, 512], P(None, None, 'tm'), may hold values from -0.1875 to 0.1875
- projection: bfloat16 [512, 960], P('tm'), may hold values from -0.25 to 0.25
- pos_weight: bfloat16 [128, 8, 120, 120], P(None, 'grp'), may hold values from -0.046875 to 0.046875
- pos_bias: bfloat16 [960], P('grp'), may hold values from -4 to 4
- cotangent: bfloat16 [1024, 960], P('tm', 'grp'), may hold values from -6 to 6
Outputs:
- encoded: bfloat16 [1024, 960], P('tm', 'grp')
- feature_grad: bfloat16 [1024, 512], P(('tm', 'grp'))
- projection_grad: float32 [512, 960], P('tm', 'grp')
The draws below stay inside these ranges and needn't reach their ends.
All inputs are finite; a program needn't handle non-finite values.
Results may differ from the reference program's by a relative error of at most 0.0085.
Values may be sent and summed in bfloat16 or wider, within the bound.
No kernel may reach another device: no remote copies, remote signals or barrier semaphores. Data moves between devices by JAX's collectives and lax.ppermute only.
A program may use at most 192 MiB of HBM per device.

```python
import math
import jax
import jax.numpy as jnp
from jax import lax

C = 512
CG = 120
GROUPS = 8
KER = 128
CH = 960
FRAMES = 1024
RECS = 1
REC_LEN = 1024


def level_of(rng, extent, cuts, smallest, high):
    def one(axis_at, parts):
        draws = jax.random.uniform(jax.random.fold_in(jax.random.fold_in(rng, 6), axis_at), (parts,), jnp.float32, smallest / len(cuts), high / len(cuts))
        return jnp.repeat(jnp.exp(draws), extent[axis_at] // parts).reshape((-1,) + (1,) * (len(extent) - axis_at - 1))

    loudness = one(*cuts[0])
    for cut in cuts[1:]:
        loudness = loudness * one(*cut)
    return loudness


def bell_draw(own_key, shape, deviation, limit, pieces=(), kind=jnp.bfloat16):
    array = jax.random.normal(own_key, shape, jnp.float32) * deviation
    if len(pieces) > 0:
        array = level_of(own_key, shape, pieces, -0.22, 0.18) * array
    return jnp.clip(array, min=-limit, max=limit).astype(kind)


def setup_inputs(seed: int = 0) -> dict:
    key_list = jax.random.split(jax.random.key(seed), 8)
    return {
        "features": bell_draw(key_list[0], (4 * FRAMES, C), 1.0, 6.0, ((0, 32),)),
        "weight_five": bell_draw(key_list[1], (2, C, C), (2 * C) ** -0.5, 0.1875, ((2, 16),)),
        "weight_six": bell_draw(key_list[2], (2, C, C), (2 * C) ** -0.5, 0.1875, ((2, 16),)),
        "projection": bell_draw(key_list[3], (C, CH), C ** -0.5, 0.25, ((0, 16),)),
        "pos_weight": bell_draw(key_list[4], (KER, GROUPS, CG, CG), (KER * CG) ** -0.5, 0.046875, ((1, 2),)),
        "pos_bias": bell_draw(key_list[5], (CH,), 1.0, 4.0, ((0, 2),)),
        "cotangent": bell_draw(key_list[6], (FRAMES, CH), 1.0, 6.0, ((0, 16), (1, 2))),
    }


epsilon = 1e-05

def normalize(values):
    average = lax.optimization_barrier(jnp.mean(values, axis=-1, keepdims=True))
    centred = values - average
    inv_dev = lax.rsqrt(lax.optimization_barrier(jnp.mean(centred * centred, axis=-1, keepdims=True)) + epsilon)
    return (centred * inv_dev, inv_dev)

def gelu_exact(values):
    return jax.nn.gelu(values, approximate=False)

def gelu_slope(values):
    normal_cdf = 0.5 * (1.0 + lax.erf(values * 0.7071067811865476))
    return normal_cdf + values * jnp.exp(-0.5 * values * values) * 0.3989422804014327

def strided_layer(inputs, weight):
    half_rows = inputs.shape[0] // 2
    paired = inputs.reshape(half_rows, 2 * inputs.shape[1])
    flat_weight = weight.reshape(2 * inputs.shape[1], weight.shape[2])
    mixed_rows = jnp.dot(paired, flat_weight, preferred_element_type=jnp.float32)
    unit_rows, _ = normalize(mixed_rows)
    return gelu_exact(unit_rows).astype(jnp.bfloat16)

def reference(features, weight_five, weight_six, projection, pos_weight, pos_bias, cotangent):
    act_five = strided_layer(features, weight_five)
    act_six = strided_layer(act_five, weight_six)
    unit, inv_dev = normalize(act_six.astype(jnp.float32))
    normed = unit.astype(jnp.bfloat16)
    hidden = jnp.dot(normed, projection, preferred_element_type=jnp.float32).astype(jnp.bfloat16)
    half_ker = KER // 2
    tap_weights = pos_weight.astype(jnp.float32)
    grouped = hidden.astype(jnp.float32).reshape(RECS, REC_LEN, GROUPS, CG)
    padded = jnp.pad(grouped, ((0, 0), (half_ker, half_ker), (0, 0), (0, 0)))

    def add_tap(summed, tap_index):
        window = lax.dynamic_slice_in_dim(padded, tap_index, REC_LEN, 1)
        return (summed + jnp.einsum('rtgi,gio->rtgo', window, tap_weights[tap_index]), None)
    zeroed = jnp.zeros((RECS, REC_LEN, GROUPS, CG), jnp.float32)
    summed, _ = lax.scan(add_tap, zeroed, jnp.arange(KER, dtype=jnp.int32))
    pos = summed.reshape(FRAMES, CH) + pos_bias.astype(jnp.float32)
    encoded = (hidden.astype(jnp.float32) + gelu_exact(pos)).astype(jnp.bfloat16)
    slope_grad = (cotangent.astype(jnp.float32) * gelu_slope(pos)).astype(jnp.bfloat16)
    grad_grouped = slope_grad.astype(jnp.float32).reshape(RECS, REC_LEN, GROUPS, CG)
    grad_padded = jnp.pad(grad_grouped, ((0, 0), (half_ker, half_ker), (0, 0), (0, 0)))

    def back_tap(summed_back, tap_index):
        window = lax.dynamic_slice_in_dim(grad_padded, KER - tap_index, REC_LEN, 1)
        return (summed_back + jnp.einsum('rtgo,gio->rtgi', window, tap_weights[tap_index]), None)
    back, _ = lax.scan(back_tap, zeroed, jnp.arange(KER, dtype=jnp.int32))
    grad_hidden = (cotangent.astype(jnp.float32) + back.reshape(FRAMES, CH)).astype(jnp.bfloat16)
    projection_grad = jnp.dot(normed.T, grad_hidden, preferred_element_type=jnp.float32) * (1.0 / math.sqrt(FRAMES))
    grad_unit = jnp.dot(grad_hidden, projection.T, preferred_element_type=jnp.float32)
    first_mean = lax.optimization_barrier(jnp.mean(grad_unit, axis=-1, keepdims=True))
    second_mean = lax.optimization_barrier(jnp.mean(grad_unit * unit, axis=-1, keepdims=True))
    feature_grad = (inv_dev * (grad_unit - first_mean - unit * second_mean)).astype(jnp.bfloat16)
    return (encoded, feature_grad, projection_grad)
```

```python
import functools
import math

import jax
import jax.numpy as jnp
from jax import lax
from jax.experimental import pallas as pl
from jax.experimental.pallas import tpu as pltpu
from jax.sharding import PartitionSpec as P

EPS = 1e-05
F32 = jnp.float32
BF16 = jnp.bfloat16
VMEM_LIMIT = 56 * 1024 * 1024


def dot_nn(a, b):
    return lax.dot_general(a, b, (((1,), (0,)), ((), ())), preferred_element_type=F32)


def dot_nt(a, b):
    return lax.dot_general(a, b, (((1,), (1,)), ((), ())), preferred_element_type=F32)


def normalize(v):
    average = jnp.mean(v, axis=-1, keepdims=True)
    centred = v - average
    inv_dev = lax.rsqrt(jnp.mean(centred * centred, axis=-1, keepdims=True) + EPS)
    return centred * inv_dev, inv_dev


def phi_cdf(v):
    return 0.5 * (1.0 + lax.erf(v * 0.7071067811865476))


def pick_rows(rows, first):
    r = lax.broadcasted_iota(jnp.int32, (rows, 2 * rows), 0)
    c = lax.broadcasted_iota(jnp.int32, (rows, 2 * rows), 1)
    return jnp.where(c == 2 * r + first, 1.0, 0.0).astype(BF16)


def flip_rows(rows):
    r = lax.broadcasted_iota(jnp.int32, (rows, rows), 0)
    c = lax.broadcasted_iota(jnp.int32, (rows, rows), 1)
    return jnp.where(c == rows - 1 - r, 1.0, 0.0).astype(BF16)


def place_taps(idx, bases, offs, pieces, full):
    for base, ref in zip(bases, pieces):
        for q, off in enumerate(offs):
            width = ref.shape[2]
            at = pl.multiple_of((idx ^ (base ^ off)) * width, width)
            for tap in range(2):
                full[tap, pl.ds(at, width), :] = ref[q, tap]


def place_rows(idx, bases, offs, pieces, full):
    for base, ref in zip(bases, pieces):
        for q, off in enumerate(offs):
            width = ref.shape[1]
            at = pl.multiple_of((idx ^ (base ^ off)) * width, width)
            full[pl.ds(at, width), :] = ref[q]


def strided(blocks, full):
    rows = blocks[0].shape[0] // 2
    even = [dot_nn(pick_rows(rows, 0), b).astype(BF16) for b in blocks]
    odd = [dot_nn(pick_rows(rows, 1), b).astype(BF16) for b in blocks]
    even, odd = jnp.concatenate(even, 0), jnp.concatenate(odd, 0)
    mixed = dot_nt(even, full[0]) + dot_nt(odd, full[1])
    unit, _ = normalize(mixed)
    return (unit * phi_cdf(unit)).astype(BF16)


def five_body(where, *refs, bases, offs, count):
    blocks, pieces = refs[:count], refs[count : count + len(bases)]
    out, full = refs[count + len(bases) :]
    place_taps(where[0], bases, offs, pieces, full)
    out[...] = strided([b[...] for b in blocks], full)


def six_body(where, act, *refs, bases, offs, count):
    pieces = refs[: len(bases)]
    normed, unit_own, inv_own, full = refs[len(bases) :]
    place_taps(where[0], bases, offs, pieces, full)
    rows = act.shape[0] // count
    act_six = strided([act[e * rows : (e + 1) * rows] for e in range(count)], full)
    unit, inv_dev = normalize(act_six.astype(F32))
    own = rows // 2
    for e in range(count):
        at = pl.multiple_of((where[1] ^ e) * own, own)
        normed[pl.ds(at, own), :] = unit[e * own : (e + 1) * own].astype(BF16)
    unit_own[...] = unit[:own]
    inv_own[...] = jnp.broadcast_to(inv_dev[:own], inv_own.shape)


def start_taps(w_any, w_vmem, sems):
    count = sems.shape[0]
    size = w_vmem.shape[0] // count

    def start(c, carry):
        pltpu.make_async_copy(
            w_any.at[pl.ds(c * size, size)], w_vmem.at[pl.ds(c * size, size)], sems.at[c]
        ).start()
        return carry

    lax.fori_loop(0, count, start, 0)


def conv_taps(w_any, w_vmem, sems, first, wrap, acc, chunk, sub):
    count = sems.shape[0]
    size = w_vmem.shape[0] // count
    groups = acc.shape[0]
    rows = acc.shape[1]
    taps = w_vmem.shape[2]
    per_group = count // groups
    s = lax.broadcasted_iota(jnp.int32, (rows, taps), 0)
    j = lax.broadcasted_iota(jnp.int32, (rows, taps), 1)
    mask = j < rows - 1 - s
    acc[...] = jnp.zeros_like(acc)

    def step(c, carry):
        if chunk == 0:
            pltpu.make_async_copy(
                w_any.at[pl.ds(c * size, size)], w_vmem.at[pl.ds(c * size, size)], sems.at[c]
            ).wait()
        total = acc[c // per_group]
        for b in range(0, size, sub):
            parts, weights = [], []
            at = pl.multiple_of(c * size + b, 8)
            f8, r8 = first[pl.ds(at, sub), :], wrap[pl.ds(at, sub), :]
            for i in range(sub):
                u = jnp.where(mask, r8[i : i + 1], f8[i : i + 1])
                u = pltpu.roll(u, taps - (rows - 1), 1, stride=1, stride_axis=0)
                parts.append(u.astype(BF16))
                weights.append(w_vmem[at + i])
            total = total + dot_nt(jnp.concatenate(parts, 1), jnp.concatenate(weights, 1))
        acc[c // per_group] = total
        return carry

    lax.fori_loop(0, count, step, 0)
    return jnp.concatenate([acc[g] for g in range(groups)], 1)


def forward_body(where, normed, got_a, got_b, *refs, bases, offs):
    pieces = refs[: len(bases)]
    w_any, cot, bias, encoded, slope_rev, proj, w_vmem, first, wrap, acc, sems = refs[len(bases) :]
    start_taps(w_any, w_vmem, sems)
    place_rows(where[0], bases, offs, pieces, proj)
    odd = where[0] % 2 == 1
    low = jnp.where(odd, got_a[...], got_b[...])
    high = jnp.where(odd, got_b[...], got_a[...])
    rows = got_a.shape[0]
    chunks = normed.shape[0] // rows
    ext = jnp.concatenate([low, normed[...], high], 0)
    hidden = dot_nn(ext, proj[...]).astype(BF16).astype(F32)
    part = lambda c: hidden[c * rows : (c + 1) * rows]
    flip = flip_rows(rows)
    for c in range(chunks):
        first[...] = jnp.concatenate([part(c), part(c + 1)], 0).T
        wrap[...] = jnp.concatenate([part(c + 2), part(c + 1)], 0).T
        pos = conv_taps(w_any, w_vmem, sems, first, wrap, acc, c, 8) + bias[...]
        cdf = phi_cdf(pos)
        here = slice(c * rows, (c + 1) * rows)
        cot_rev = dot_nn(flip, cot[here, :])
        hid_rev = dot_nn(flip, part(c + 1).astype(BF16))
        enc_rev = (hid_rev + pos * cdf).astype(BF16)
        encoded[here, :] = dot_nn(flip, enc_rev).astype(BF16)
        slope = cdf + pos * jnp.exp(-0.5 * pos * pos) * 0.3989422804014327
        slope_rev[here, :] = (cot_rev * slope).astype(BF16)


def backward_body(where, slope_rev, got_a, got_b, w_any, cot, normed, proj, *refs, scale):
    part_grad, unit_grad, w_vmem, first, wrap, acc, hid_grad, full, sems = refs
    start_taps(w_any, w_vmem, sems)
    odd = where[0] % 2 == 1
    low = jnp.where(odd, got_a[...], got_b[...])
    high = jnp.where(odd, got_b[...], got_a[...])
    rows = got_a.shape[0]
    chunks = slope_rev.shape[0] // rows
    ext = jnp.concatenate([low, slope_rev[...], high], 0).astype(F32)
    part = lambda c: ext[c * rows : (c + 1) * rows]
    for c in range(chunks):
        first[...] = jnp.concatenate([part(c + 2), part(c + 1)], 0).T
        wrap[...] = jnp.concatenate([part(c), part(c + 1)], 0).T
        back = conv_taps(w_any, w_vmem, sems, first, wrap, acc, c, 8)
        here = slice(c * rows, (c + 1) * rows)
        hid_grad[here, :] = (cot[here, :].astype(F32) + back).astype(BF16)
    grad = hid_grad[...]
    members, width = full.shape[0], full.shape[1]
    full[...] = (
        dot_nn(normed[...].astype(F32).T.astype(BF16), grad) * scale
    ).reshape(full.shape)
    for p in range(members):
        part_grad[p] = full[where[0] ^ p].astype(BF16)
    unit_grad[...] = dot_nt(grad, proj[...])


def vmem_specs(count):
    return [pl.BlockSpec(memory_space=pltpu.VMEM)] * count


SMEM_SPEC = pl.BlockSpec(memory_space=pltpu.SMEM)
ANY_SPEC = pl.BlockSpec(memory_space=pl.ANY)
PARAMS = pltpu.CompilerParams(vmem_limit_bytes=VMEM_LIMIT)


def swap(values, axis, mask):
    count = lax.axis_size(axis)
    return lax.ppermute(values, axis, [(i, i ^ mask) for i in range(count)])


def spread(shard, count):
    offs = [0, count // 4, count // 2, 3 * (count // 4)]
    stack = jnp.concatenate([shard[None]] + [swap(shard, "tm", m)[None] for m in offs[1:]], 0)
    stacks, bases = [stack], [0]
    mask = count // 8
    while mask >= 1:
        stacks = stacks + [swap(s, "tm", mask) for s in stacks]
        bases = bases + [b ^ mask for b in bases]
        mask //= 2
    return stacks, bases, offs


def halo(tail, head, parity):
    count = lax.axis_size("tm")
    to_a = tail if tail is head else jnp.where(parity == 0, tail, head)
    to_b = tail if tail is head else jnp.where(parity == 0, head, tail)
    pairs = [(2 * i + 1, 2 * i + 2) for i in range(count // 2 - 1)]
    got_b = lax.ppermute(to_b, "tm", pairs + [(b, a) for a, b in pairs])
    return swap(to_a, "tm", 1), got_b


def on_device(features, weight_five, weight_six, projection, pos_weight, pos_bias, cotangent):
    members, slots = lax.axis_size("tm"), lax.axis_size("grp")
    me, slot = lax.axis_index("tm"), lax.axis_index("grp")
    where = jnp.stack([me, slot]).astype(jnp.int32)
    channels = features.shape[1]
    taps, groups, width = pos_weight.shape[0], pos_weight.shape[1], pos_weight.shape[2]
    columns = groups * width
    half = taps // 2
    own = features.shape[0] // 4
    block = own * slots

    w_taps = jnp.transpose(pos_weight, (1, 2, 3, 0)).reshape(groups * width, width, taps)
    w_back = jnp.transpose(pos_weight, (1, 3, 2, 0)).reshape(groups * width, width, taps)

    blocks = [features] + [swap(features, "grp", e) for e in range(1, slots)]
    five, bases, offs = spread(jnp.transpose(weight_five, (0, 2, 1)), members)
    six, _, _ = spread(jnp.transpose(weight_six, (0, 2, 1)), members)
    proj_half = lax.dynamic_slice_in_dim(projection, slot * columns, columns, 1)
    proj_parts, _, _ = spread(proj_half, members)
    common = dict(bases=bases, offs=offs)
    taps_scratch = pltpu.VMEM((2, channels, channels), BF16)

    act_five = pl.pallas_call(
        functools.partial(five_body, count=slots, **common),
        in_specs=[SMEM_SPEC] + vmem_specs(slots + len(five)),
        out_specs=vmem_specs(1)[0],
        out_shape=jax.ShapeDtypeStruct((2 * block, channels), BF16),
        scratch_shapes=[taps_scratch],
        compiler_params=PARAMS,
        name="five",
    )(where, *blocks, *five)
    normed, unit, inv_dev = pl.pallas_call(
        functools.partial(six_body, count=slots, **common),
        in_specs=[SMEM_SPEC] + vmem_specs(1 + len(six)),
        out_specs=vmem_specs(3),
        out_shape=[
            jax.ShapeDtypeStruct((block, channels), BF16),
            jax.ShapeDtypeStruct((own, channels), F32),
            jax.ShapeDtypeStruct((own, 128), F32),
        ],
        scratch_shapes=[taps_scratch],
        compiler_params=PARAMS,
        name="six",
    )(where, act_five, *six)

    whole = block == half
    tail = normed if whole else normed[block - half :]
    head = normed if whole else normed[:half]
    got_a, got_b = halo(tail, head, me % 2)
    copies = 5 * groups
    conv_scratch = [
        pltpu.VMEM((groups * width, width, taps), BF16),
        pltpu.VMEM((columns, taps), F32),
        pltpu.VMEM((columns, taps), F32),
        pltpu.VMEM((groups, half, width), F32),
    ]
    sems = pltpu.SemaphoreType.DMA((copies,))
    encoded, slope_rev, proj = pl.pallas_call(
        functools.partial(forward_body, **common),
        in_specs=[SMEM_SPEC]
        + vmem_specs(3 + len(proj_parts))
        + [ANY_SPEC]
        + vmem_specs(2),
        out_specs=vmem_specs(3),
        out_shape=[
            jax.ShapeDtypeStruct((block, columns), BF16),
            jax.ShapeDtypeStruct((block, columns), BF16),
            jax.ShapeDtypeStruct((channels, columns), BF16),
        ],
        scratch_shapes=conv_scratch + [sems],
        compiler_params=PARAMS,
        name="forward",
    )(
        where, normed, got_a, got_b, *proj_parts, w_taps, cotangent,
        pos_bias.astype(F32).reshape(1, columns),
    )

    tail = slope_rev if whole else slope_rev[block - half :]
    head = slope_rev if whole else slope_rev[:half]
    got_a, got_b = halo(tail, head, me % 2)
    scale = 1.0 / math.sqrt(own * members * slots)
    share = channels // members
    part_grad, unit_grad = pl.pallas_call(
        functools.partial(backward_body, scale=scale),
        in_specs=[SMEM_SPEC] + vmem_specs(3) + [ANY_SPEC] + vmem_specs(3),
        out_specs=vmem_specs(2),
        out_shape=[
            jax.ShapeDtypeStruct((members, share, columns), BF16),
            jax.ShapeDtypeStruct((block, channels), F32),
        ],
        scratch_shapes=conv_scratch
        + [
            pltpu.VMEM((block, columns), BF16),
            pltpu.VMEM((members, share, columns), F32),
            sems,
        ],
        compiler_params=PARAMS,
        name="backward",
    )(where, slope_rev, got_a, got_b, w_back, cotangent, normed, proj)

    kept, got = part_grad[0::2], swap(part_grad[1::2], "tm", 1)
    mask = members // 2
    while mask >= 2:
        total = (kept.astype(F32) + got.astype(F32)).astype(BF16)
        middle = total.shape[0] // 2
        kept, got = total[:middle], swap(total[middle:], "tm", mask)
        mask //= 2
    projection_grad = kept[0].astype(F32) + got[0].astype(F32)

    if slots == 2:
        mine = lax.dynamic_slice_in_dim(unit_grad, slot * own, own, 0)
        theirs = lax.dynamic_slice_in_dim(unit_grad, (1 - slot) * own, own, 0)
        grad_unit = mine + swap(theirs.astype(BF16), "grp", 1).astype(F32)
    else:
        grad_unit = lax.psum_scatter(unit_grad, "grp", scatter_dimension=0, tiled=True)
    first_mean = jnp.mean(grad_unit, axis=-1, keepdims=True)
    second_mean = jnp.mean(grad_unit * unit, axis=-1, keepdims=True)
    feature_grad = (inv_dev[:, :1] * (grad_unit - first_mean - unit * second_mean)).astype(BF16)
    return (encoded, feature_grad, projection_grad)


def solution(mesh):
    in_specs = (
        P(("tm", "grp"), None),
        P(None, None, "tm"),
        P(None, None, "tm"),
        P("tm", None),
        P(None, "grp", None, None),
        P("grp"),
        P("tm", "grp"),
    )
    out_specs = (P("tm", "grp"), P(("tm", "grp"), None), P("tm", "grp"))
    return jax.shard_map(
        on_device, mesh=mesh, in_specs=in_specs, out_specs=out_specs, check_vma=False
    )
```

```python
import functools
import math

import jax
import jax.numpy as jnp
from jax import lax
from jax.experimental import pallas as pl
from jax.experimental.pallas import tpu as pltpu
from jax.sharding import PartitionSpec as P


EPS = 1e-05
F32 = jnp.float32
BF16 = jnp.bfloat16
VMEM_LIMIT = 56 * 1024 * 1024


def dot_nn(a, b):
    return lax.dot_general(a, b, (((1,), (0,)), ((), ())), preferred_element_type=F32)


def dot_nt(a, b):
    return lax.dot_general(a, b, (((1,), (1,)), ((), ())), preferred_element_type=F32)


def normalize(v):
    average = jnp.mean(v, axis=-1, keepdims=True)
    centred = v - average
    inv_dev = lax.rsqrt(jnp.mean(centred * centred, axis=-1, keepdims=True) + EPS)
    return centred * inv_dev, inv_dev


def phi_cdf(v):
    return 0.5 * (1.0 + lax.erf(v * 0.7071067811865476))


def pick_rows(rows, first):
    r = lax.broadcasted_iota(jnp.int32, (rows, 2 * rows), 0)
    c = lax.broadcasted_iota(jnp.int32, (rows, 2 * rows), 1)
    return jnp.where(c == 2 * r + first, 1.0, 0.0).astype(BF16)


def flip_rows(rows):
    r = lax.broadcasted_iota(jnp.int32, (rows, rows), 0)
    c = lax.broadcasted_iota(jnp.int32, (rows, rows), 1)
    return jnp.where(c == rows - 1 - r, 1.0, 0.0).astype(BF16)


def place_shards(idx, layout, stacks, first, taps, full, sems, base=0):
    copies = []
    for offs, ref in zip(layout, stacks):
        width = ref.shape[2]
        for q, off in enumerate(offs):
            at = pl.multiple_of((idx ^ off) * width, width)
            for tap in range(taps):
                copies.append(
                    pltpu.make_async_copy(
                        ref.at[q, first + tap],
                        full.at[tap, pl.ds(at, width), :],
                        sems.at[base + len(copies)],
                    )
                )
    for c in copies:
        c.start()
    return copies


def strided(blocks, full):
    rows = blocks[0].shape[0] // 2
    even = [dot_nn(pick_rows(rows, 0), b).astype(BF16) for b in blocks]
    odd = [dot_nn(pick_rows(rows, 1), b).astype(BF16) for b in blocks]
    even, odd = jnp.concatenate(even, 0), jnp.concatenate(odd, 0)
    mixed = dot_nt(even, full[0]) + dot_nt(odd, full[1])
    unit, _ = normalize(mixed)
    return (unit * phi_cdf(unit)).astype(BF16)


def five_body(where, *refs, layout, count):
    blocks, stacks = refs[:count], refs[count : count + len(layout)]
    out, full, sems = refs[count + len(layout) :]
    copies = place_shards(where[0], layout, stacks, 0, 2, full, sems)
    for c in copies:
        c.wait()
    out[...] = strided([b[...] for b in blocks], full)


def six_body(where, act, *refs, layout, count):
    stacks = refs[: len(layout)]
    normed, unit_own, inv_own, full, sems = refs[len(layout) :]
    copies = place_shards(where[0], layout, stacks, 0, 2, full, sems)
    for c in copies:
        c.wait()
    rows = act.shape[0] // count
    act_six = strided([act[e * rows : (e + 1) * rows] for e in range(count)], full)
    unit, inv_dev = normalize(act_six.astype(F32))
    own = rows // 2
    for e in range(count):
        at = pl.multiple_of((where[1] ^ e) * own, own)
        normed[pl.ds(at, own), :] = unit[e * own : (e + 1) * own].astype(BF16)
    unit_own[...] = unit[:own]
    inv_own[...] = jnp.broadcast_to(inv_dev[:own], inv_own.shape)


def swap_channels_body(w_ref, out_ref):
    out_ref[...] = jnp.swapaxes(w_ref[0], 0, 1)


def swap_channels(weights, group):
    a, b, taps = weights.shape[1:]
    size = 2 * a * b * taps
    return pl.pallas_call(
        swap_channels_body,
        grid=(1,),
        in_specs=[pl.BlockSpec((1, a, b, taps), lambda i: (group, 0, 0, 0))],
        out_specs=pl.BlockSpec((b, a, taps), lambda i: (0, 0, 0)),
        out_shape=jax.ShapeDtypeStruct((b, a, taps), weights.dtype),
        compiler_params=PARAMS,
        cost_estimate=pl.CostEstimate(flops=0, transcendentals=0, bytes_accessed=2 * size),
        name="swap_channels",
    )(weights)


def start_taps(w_anys, w_vmem, sems):
    per_group = sems.shape[0] // len(w_anys)
    size = w_vmem.shape[0] // sems.shape[0]
    for g, w_any in enumerate(w_anys):
        for c in range(per_group):
            at = g * per_group + c
            pltpu.make_async_copy(
                w_any.at[pl.ds(c * size, size)], w_vmem.at[pl.ds(at * size, size)], sems.at[at]
            ).start()


def conv_taps(w_vmem, sems, first, wrap, acc, chunk, sub):
    count = sems.shape[0]
    size = w_vmem.shape[0] // count
    groups = acc.shape[0]
    rows = acc.shape[1]
    taps = w_vmem.shape[2]
    per_group = count // groups
    s = lax.broadcasted_iota(jnp.int32, (rows, taps), 0)
    j = lax.broadcasted_iota(jnp.int32, (rows, taps), 1)
    mask = j < rows - 1 - s
    acc[...] = jnp.zeros_like(acc)

    def step(c, carry):
        if chunk == 0:
            here = w_vmem.at[pl.ds(c * size, size)]
            pltpu.make_async_copy(here, here, sems.at[c]).wait()
        total = acc[c // per_group]
        for b in range(0, size, sub):
            parts, weights = [], []
            at = pl.multiple_of(c * size + b, 8)
            f8, r8 = first[pl.ds(at, sub), :], wrap[pl.ds(at, sub), :]
            for i in range(sub):
                u = jnp.where(mask, r8[i : i + 1], f8[i : i + 1])
                u = pltpu.roll(u, taps - (rows - 1), 1, stride=1, stride_axis=0)
                parts.append(u.astype(BF16))
                weights.append(w_vmem[at + i])
            total = total + dot_nt(jnp.concatenate(parts, 1), jnp.concatenate(weights, 1))
        acc[c // per_group] = total
        return carry

    lax.fori_loop(0, count, step, 0)
    return jnp.concatenate([acc[g] for g in range(groups)], 1)


def forward_body(where, normed, got_a, got_b, *refs, layout, groups):
    stacks = refs[: len(layout)]
    w_any, cot, bias, encoded, slope_rev, proj = refs[len(layout) : len(layout) + 6]
    w_vmem, first, wrap, acc, full, sems, proj_sems = refs[len(layout) + 6 :]
    copies = place_shards(where[0], layout, stacks, 2, 1, full, proj_sems)
    start_taps([w_any.at[g] for g in range(groups)], w_vmem, sems)
    for c in copies:
        c.wait()
    proj[...] = full[0, :, : proj.shape[1]]
    odd = where[0] % 2 == 1
    low = jnp.where(odd, got_a[...], got_b[...])
    high = jnp.where(odd, got_b[...], got_a[...])
    rows = got_a.shape[0]
    chunks = normed.shape[0] // rows
    ext = jnp.concatenate([low, normed[...], high], 0)
    hidden = dot_nn(ext, proj[...]).astype(BF16).astype(F32)
    part = lambda c: hidden[c * rows : (c + 1) * rows]
    flip = flip_rows(rows)
    for c in range(chunks):
        first[...] = jnp.concatenate([part(c), part(c + 1)], 0).T
        wrap[...] = jnp.concatenate([part(c + 2), part(c + 1)], 0).T
        pos = conv_taps(w_vmem, sems, first, wrap, acc, c, 8)
        pos = pos + bias[...].astype(F32)
        cdf = phi_cdf(pos)
        here = slice(c * rows, (c + 1) * rows)
        cot_rev = dot_nn(flip, cot[here, :])
        hid_rev = dot_nn(flip, part(c + 1).astype(BF16))
        enc_rev = (hid_rev + pos * cdf).astype(BF16)
        encoded[here, :] = dot_nn(flip, enc_rev).astype(BF16)
        slope = cdf + pos * jnp.exp(-0.5 * pos * pos) * 0.3989422804014327
        slope_rev[here, :] = (cot_rev * slope).astype(BF16)


def backward_body(where, slope_rev, got_a, got_b, *refs, scale, order, groups):
    w_anys = refs[:groups]
    cot, normed, proj, kept, sent, unit_grad, w_vmem, first, wrap, acc, hid_grad, full, rows_f32, sems = refs[groups:]
    start_taps(w_anys, w_vmem, sems)
    odd = where[0] % 2 == 1
    low = jnp.where(odd, got_a[...], got_b[...])
    high = jnp.where(odd, got_b[...], got_a[...])
    rows = got_a.shape[0]
    chunks = slope_rev.shape[0] // rows
    ext = jnp.concatenate([low, slope_rev[...], high], 0).astype(F32)
    part = lambda c: ext[c * rows : (c + 1) * rows]
    for c in range(chunks):
        first[...] = jnp.concatenate([part(c + 2), part(c + 1)], 0).T
        wrap[...] = jnp.concatenate([part(c), part(c + 1)], 0).T
        back = conv_taps(w_vmem, sems, first, wrap, acc, c, 8)
        here = slice(c * rows, (c + 1) * rows)
        hid_grad[here, :] = (cot[here, :].astype(F32) + back).astype(BF16)
    grad = hid_grad[...]
    full[...] = (
        dot_nn(normed[...].astype(F32).T.astype(BF16), grad) * scale
    ).reshape(full.shape)
    for n, p in enumerate(order):
        kept[n] = full[where[0] ^ p].astype(BF16)
        sent[n] = full[where[0] ^ (p ^ 1)].astype(BF16)
    slots = unit_grad.shape[0]
    rows_f32[...] = dot_nt(grad, proj[...]).reshape(rows_f32.shape)
    for e in range(slots):
        unit_grad[e] = rows_f32[where[1] ^ e]


def vmem_specs(count):
    return [pl.BlockSpec(memory_space=pltpu.VMEM)] * count


SMEM_SPEC = pl.BlockSpec(memory_space=pltpu.SMEM)
ANY_SPEC = pl.BlockSpec(memory_space=pl.ANY)
PARAMS = pltpu.CompilerParams(vmem_limit_bytes=VMEM_LIMIT)


def swap(values, axis, mask):
    count = lax.axis_size(axis)
    return lax.ppermute(values, axis, [(i, i ^ mask) for i in range(count)])


def spread(shard, count):
    stack, offs = shard[None], [0]
    mask = count // 2
    while mask >= 4:
        got = swap(stack, "tm", mask)
        stack = jnp.concatenate([stack, got], 0)
        offs = offs + [o ^ mask for o in offs]
        mask //= 2
    stacks, layout = [stack], [offs]
    for mask in (2, 1):
        stacks = stacks + [swap(s, "tm", mask) for s in stacks]
        layout = layout + [[o ^ mask for o in offs] for offs in layout]
    return stacks, layout


def halo(tail, head, parity):
    count = lax.axis_size("tm")
    to_a = tail if tail is head else jnp.where(parity == 0, tail, head)
    to_b = tail if tail is head else jnp.where(parity == 0, head, tail)
    pairs = [(2 * i + 1, 2 * i + 2) for i in range(count // 2 - 1)]
    got_b = lax.ppermute(to_b, "tm", pairs + [(b, a) for a, b in pairs])
    return swap(to_a, "tm", 1), got_b


def on_device(features, weight_five, weight_six, projection, pos_weight, pos_bias, cotangent):
    members, slots = lax.axis_size("tm"), lax.axis_size("grp")
    me, slot = lax.axis_index("tm"), lax.axis_index("grp")
    where = jnp.stack([me, slot]).astype(jnp.int32)
    channels = features.shape[1]
    taps, groups, width = pos_weight.shape[0], pos_weight.shape[1], pos_weight.shape[2]
    columns = groups * width
    half = taps // 2
    own = features.shape[0] // 4
    block = own * slots

    w_taps = jnp.transpose(pos_weight, (1, 2, 3, 0))
    w_back = []
    for g in range(groups):
        w_back.append(swap_channels(w_taps, g))

    blocks = [features] + [swap(features, "grp", e) for e in range(1, slots)]
    five, layout = spread(jnp.transpose(weight_five, (0, 2, 1)), members)
    proj_half = lax.dynamic_slice_in_dim(projection, slot * columns, columns, 1)
    proj_half = jnp.pad(proj_half, ((0, 0), (0, channels - columns)))
    rest, _ = spread(
        jnp.concatenate([jnp.transpose(weight_six, (0, 2, 1)), proj_half[None]], 0), members
    )
    common = dict(layout=layout)
    taps_scratch = [
        pltpu.VMEM((2, channels, channels), BF16),
        pltpu.SemaphoreType.DMA((2 * members,)),
    ]
    act_five = pl.pallas_call(
        functools.partial(five_body, count=slots, **common),
        in_specs=[SMEM_SPEC] + vmem_specs(slots) + [ANY_SPEC] * len(five),
        out_specs=vmem_specs(1)[0],
        out_shape=jax.ShapeDtypeStruct((2 * block, channels), BF16),
        scratch_shapes=taps_scratch,
        compiler_params=PARAMS,
        name="five",
    )(where, *blocks, *five)
    normed, unit, inv_dev = pl.pallas_call(
        functools.partial(six_body, count=slots, **common),
        in_specs=[SMEM_SPEC] + vmem_specs(1) + [ANY_SPEC] * len(rest),
        out_specs=vmem_specs(3),
        out_shape=[
            jax.ShapeDtypeStruct((block, channels), BF16),
            jax.ShapeDtypeStruct((own, channels), F32),
            jax.ShapeDtypeStruct((own, 128), F32),
        ],
        scratch_shapes=taps_scratch,
        compiler_params=PARAMS,
        name="six",
    )(where, act_five, *rest)

    whole = block == half
    tail = normed if whole else normed[block - half :]
    head = normed if whole else normed[:half]
    got_a, got_b = halo(tail, head, me % 2)
    copies = 5 * groups
    conv_scratch = [
        pltpu.VMEM((groups * width, width, taps), BF16),
        pltpu.VMEM((columns, taps), F32),
        pltpu.VMEM((columns, taps), F32),
        pltpu.VMEM((groups, half, width), F32),
    ]
    sems = pltpu.SemaphoreType.DMA((copies,))
    encoded, slope_rev, proj = pl.pallas_call(
        functools.partial(forward_body, groups=groups, **common),
        in_specs=[SMEM_SPEC] + vmem_specs(3) + [ANY_SPEC] * (len(rest) + 1) + vmem_specs(2),
        out_specs=vmem_specs(3),
        out_shape=[
            jax.ShapeDtypeStruct((block, columns), BF16),
            jax.ShapeDtypeStruct((block, columns), BF16),
            jax.ShapeDtypeStruct((channels, columns), BF16),
        ],
        scratch_shapes=conv_scratch
        + [pltpu.VMEM((1, channels, channels), BF16), sems, pltpu.SemaphoreType.DMA((members,))],
        compiler_params=PARAMS,
        name="forward",
    )(
        where, normed, got_a, got_b, *rest, w_taps, cotangent, pos_bias.reshape(1, columns),
    )

    tail = slope_rev if whole else slope_rev[block - half :]
    head = slope_rev if whole else slope_rev[:half]
    got_a, got_b = halo(tail, head, me % 2)
    scale = 1.0 / math.sqrt(own * members * slots)
    share = channels // members
    finals = [0, members // 4, members // 2, 3 * (members // 4)]
    masks, mask = [], 2
    while mask < members // 4:
        masks.append(mask)
        mask *= 2
    order = finals
    for mask in reversed(masks):
        order = order + [p ^ mask for p in order]
    kept, sent, unit_grad = pl.pallas_call(
        functools.partial(backward_body, scale=scale, order=order, groups=groups),
        in_specs=[SMEM_SPEC] + vmem_specs(3) + [ANY_SPEC] * groups + vmem_specs(3),
        out_specs=vmem_specs(3),
        out_shape=[jax.ShapeDtypeStruct((members // 2, share, columns), BF16)] * 2
        + [jax.ShapeDtypeStruct((slots, own, channels), F32)],
        scratch_shapes=conv_scratch
        + [
            pltpu.VMEM((block, columns), BF16),
            pltpu.VMEM((members, share, columns), F32),
            pltpu.VMEM((slots, own, channels), F32),
            sems,
        ],
        compiler_params=PARAMS,
        name="backward",
    )(where, slope_rev, got_a, got_b, *w_back, cotangent, normed, proj)

    total = (kept.astype(F32) + swap(sent, "tm", 1).astype(F32)).astype(BF16)
    for mask in masks:
        middle = total.shape[0] // 2
        got = swap(total[middle:], "tm", mask)
        total = (total[:middle].astype(F32) + got.astype(F32)).astype(BF16)
    parts = [swap(total[n], "tm", p) for n, p in enumerate(finals) if p]
    projection_grad = total[0].astype(F32) + sum(p.astype(F32) for p in parts)

    grad_unit = unit_grad[0]
    for e in range(1, slots):
        grad_unit = grad_unit + swap(unit_grad[e].astype(BF16), "grp", e).astype(F32)
    first_mean = jnp.mean(grad_unit, axis=-1, keepdims=True)
    second_mean = jnp.mean(grad_unit * unit, axis=-1, keepdims=True)
    feature_grad = (inv_dev[:, :1] * (grad_unit - first_mean - unit * second_mean)).astype(BF16)
    return (encoded, feature_grad, projection_grad)


def solution(mesh):
    in_specs = (
        P(("tm", "grp"), None),
        P(None, None, "tm"),
        P(None, None, "tm"),
        P("tm", None),
        P(None, "grp", None, None),
        P("grp"),
        P("tm", "grp"),
    )
    out_specs = (P("tm", "grp"), P(("tm", "grp"), None), P("tm", "grp"))

    return jax.shard_map(
        on_device, mesh=mesh, in_specs=in_specs, out_specs=out_specs, check_vma=False
    )
```

```python
import functools
import math

import jax
import jax.numpy as jnp
from jax import lax
from jax.experimental import pallas as pl
from jax.experimental.pallas import tpu as pltpu
from jax.sharding import PartitionSpec as P


EPS = 1e-05
F32 = jnp.float32
BF16 = jnp.bfloat16
VMEM_LIMIT = 56 * 1024 * 1024
SUB = 8


def dot_nn(a, b):
    return lax.dot_general(a, b, (((1,), (0,)), ((), ())), preferred_element_type=F32)


def dot_nt(a, b):
    return lax.dot_general(a, b, (((1,), (1,)), ((), ())), preferred_element_type=F32)


def normalize(v):
    average = jnp.mean(v, axis=-1, keepdims=True)
    centred = v - average
    inv_dev = lax.rsqrt(jnp.mean(centred * centred, axis=-1, keepdims=True) + EPS)
    return centred * inv_dev, inv_dev


def phi_cdf(v):
    return 0.5 * (1.0 + lax.erf(v * 0.7071067811865476))


def pick_rows(rows, first):
    r = lax.broadcasted_iota(jnp.int32, (rows, 2 * rows), 0)
    c = lax.broadcasted_iota(jnp.int32, (rows, 2 * rows), 1)
    return jnp.where(c == 2 * r + first, 1.0, 0.0).astype(BF16)


def flip_rows(rows):
    r = lax.broadcasted_iota(jnp.int32, (rows, rows), 0)
    c = lax.broadcasted_iota(jnp.int32, (rows, rows), 1)
    return jnp.where(c == rows - 1 - r, 1.0, 0.0).astype(BF16)


def place_shards(idx, layout, stacks, first, taps, full):
    for offs, ref in zip(layout, stacks):
        width = ref.shape[2]
        for q, off in enumerate(offs):
            at = pl.multiple_of((idx ^ off) * width, width)
            for tap in range(taps):
                full[tap, pl.ds(at, width), :] = ref[q, first + tap]


def strided(blocks, full):
    rows = blocks[0].shape[0] // 2
    even = [dot_nn(pick_rows(rows, 0), b).astype(BF16) for b in blocks]
    odd = [dot_nn(pick_rows(rows, 1), b).astype(BF16) for b in blocks]
    even, odd = jnp.concatenate(even, 0), jnp.concatenate(odd, 0)
    mixed = dot_nt(even, full[0]) + dot_nt(odd, full[1])
    unit, _ = normalize(mixed)
    return (unit * phi_cdf(unit)).astype(BF16)


def five_body(where, *refs, layout, count):
    blocks, stacks = refs[:count], refs[count : count + len(layout)]
    out, full = refs[count + len(layout) :]
    place_shards(where[0], layout, stacks, 0, 2, full)
    out[...] = strided([b[...] for b in blocks], full)


def six_body(where, act, *refs, layout, count):
    stacks = refs[: len(layout)]
    normed, unit_own, inv_own, full = refs[len(layout) :]
    place_shards(where[0], layout, stacks, 0, 2, full)
    rows = act.shape[0] // count
    act_six = strided([act[e * rows : (e + 1) * rows] for e in range(count)], full)
    unit, inv_dev = normalize(act_six.astype(F32))
    own = rows // 2
    for e in range(count):
        at = pl.multiple_of((where[1] ^ e) * own, own)
        normed[pl.ds(at, own), :] = unit[e * own : (e + 1) * own].astype(BF16)
    unit_own[...] = unit[:own]
    inv_own[...] = jnp.broadcast_to(inv_dev[:own], inv_own.shape)


def project_body(where, *refs, layout):
    stacks = refs[: len(layout)]
    proj, full, sems = refs[len(layout) :]
    copies = []
    for offs, ref in zip(layout, stacks):
        width = ref.shape[2]
        for q, off in enumerate(offs):
            at = pl.multiple_of((where[0] ^ off) * width, width)
            copies.append(
                pltpu.make_async_copy(
                    ref.at[q, 2], full.at[pl.ds(at, width), :], sems.at[len(copies)]
                )
            )
    for c in copies:
        c.start()
    for c in copies:
        c.wait()
    proj[...] = full[:, : proj.shape[1]]


def start_taps(w_any, w_vmem, sems):
    def start(g, carry):
        tap_copy(w_any, w_vmem, sems, g).start()
        return carry

    lax.fori_loop(0, w_vmem.shape[0], start, 0)


def tap_copy(w_any, w_vmem, sems, g):
    return pltpu.make_async_copy(w_any.at[g], w_vmem.at[g], sems.at[g])


def conv_group(weights, first, wrap, rows):
    size, _, taps = weights.shape
    s = lax.broadcasted_iota(jnp.int32, (rows, taps), 0)
    j = lax.broadcasted_iota(jnp.int32, (rows, taps), 1)
    mask = j < rows - 1 - s
    total = None
    for b in range(0, size, SUB):
        parts = []
        for i in range(b, b + SUB):
            u = jnp.where(mask, wrap[i : i + 1, :], first[i : i + 1, :])
            u = pltpu.roll(u, taps - (rows - 1), 1, stride=1, stride_axis=0)
            parts.append(u.astype(BF16))
        tiles = [weights[i] for i in range(b, b + SUB)]
        term = dot_nt(jnp.concatenate(parts, 1), jnp.concatenate(tiles, 1))
        total = term if total is None else total + term
    return total


def conv(w_any, w_vmem, turned, sems, first, wrap, acc, chunk):
    groups, width = w_vmem.shape[:2]
    rows = acc.shape[1]

    def step(g, carry):
        if chunk == 0:
            tap_copy(w_any, w_vmem, sems, g).wait()
        weights = w_vmem.at[g]
        if turned is not None:
            turned[...] = jnp.swapaxes(w_vmem[g], 0, 1)
            weights = turned
        here = pl.ds(pl.multiple_of(g * width, 8), width)
        acc[g] = conv_group(weights, first.at[here], wrap.at[here], rows)
        return carry

    lax.fori_loop(0, groups, step, 0)
    return jnp.concatenate([acc[g] for g in range(groups)], 1)


def forward_body(where, normed, got_a, got_b, proj, w_any, cot, bias, *refs):
    encoded, slope_rev, w_vmem, first, wrap, acc, sems = refs
    start_taps(w_any, w_vmem, sems)
    odd = where[0] % 2 == 1
    low = jnp.where(odd, got_a[...], got_b[...])
    high = jnp.where(odd, got_b[...], got_a[...])
    rows = got_a.shape[0]
    chunks = normed.shape[0] // rows
    ext = jnp.concatenate([low, normed[...], high], 0)
    hidden = dot_nn(ext, proj[...]).astype(BF16).astype(F32)
    part = lambda c: hidden[c * rows : (c + 1) * rows]
    flip = flip_rows(rows)
    for c in range(chunks):
        first[...] = jnp.concatenate([part(c), part(c + 1)], 0).T
        wrap[...] = jnp.concatenate([part(c + 2), part(c + 1)], 0).T
        pos = conv(w_any, w_vmem, None, sems, first, wrap, acc, c)
        pos = pos + bias[...].astype(F32)
        cdf = phi_cdf(pos)
        here = slice(c * rows, (c + 1) * rows)
        cot_rev = dot_nn(flip, cot[here, :])
        hid_rev = dot_nn(flip, part(c + 1).astype(BF16))
        enc_rev = (hid_rev + pos * cdf).astype(BF16)
        encoded[here, :] = dot_nn(flip, enc_rev).astype(BF16)
        slope = cdf + pos * jnp.exp(-0.5 * pos * pos) * 0.3989422804014327
        slope_rev[here, :] = (cot_rev * slope).astype(BF16)


def backward_body(where, slope_rev, got_a, got_b, w_any, cot, normed, proj, *refs, scale, order):
    kept, sent, unit_grad, w_vmem, first, wrap, acc, sems = refs[:8]
    turned, hid_grad, full, rows_f32 = refs[8:]
    start_taps(w_any, w_vmem, sems)
    odd = where[0] % 2 == 1
    low = jnp.where(odd, got_a[...], got_b[...])
    high = jnp.where(odd, got_b[...], got_a[...])
    rows = got_a.shape[0]
    chunks = slope_rev.shape[0] // rows
    ext = jnp.concatenate([low, slope_rev[...], high], 0).astype(F32)
    part = lambda c: ext[c * rows : (c + 1) * rows]
    for c in range(chunks):
        first[...] = jnp.concatenate([part(c + 2), part(c + 1)], 0).T
        wrap[...] = jnp.concatenate([part(c), part(c + 1)], 0).T
        back = conv(w_any, w_vmem, turned, sems, first, wrap, acc, c)
        here = slice(c * rows, (c + 1) * rows)
        hid_grad[here, :] = (cot[here, :].astype(F32) + back).astype(BF16)
    grad = hid_grad[...]
    full[...] = (
        dot_nn(normed[...].astype(F32).T.astype(BF16), grad) * scale
    ).reshape(full.shape)
    for n, p in enumerate(order):
        kept[n] = full[where[0] ^ p].astype(BF16)
        sent[n] = full[where[0] ^ (p ^ 1)].astype(BF16)
    slots = unit_grad.shape[0]
    rows_f32[...] = dot_nt(grad, proj[...]).reshape(rows_f32.shape)
    for e in range(slots):
        unit_grad[e] = rows_f32[where[1] ^ e]


def vmem_specs(count):
    return [pl.BlockSpec(memory_space=pltpu.VMEM)] * count


SMEM_SPEC = pl.BlockSpec(memory_space=pltpu.SMEM)
ANY_SPEC = pl.BlockSpec(memory_space=pl.ANY)
PARAMS = pltpu.CompilerParams(vmem_limit_bytes=VMEM_LIMIT)


def swap(values, axis, mask):
    count = lax.axis_size(axis)
    return lax.ppermute(values, axis, [(i, i ^ mask) for i in range(count)])


def spread(shard, count):
    stack, offs = shard[None], [0]
    mask = count // 2
    while mask >= 4:
        got = swap(stack, "tm", mask)
        stack = jnp.concatenate([stack, got], 0)
        offs = offs + [o ^ mask for o in offs]
        mask //= 2
    stacks, layout = [stack], [offs]
    for mask in (2, 1):
        stacks = stacks + [swap(s, "tm", mask) for s in stacks]
        layout = layout + [[o ^ mask for o in offs] for offs in layout]
    return stacks, layout


def halo(tail, head, parity):
    count = lax.axis_size("tm")
    to_a = tail if tail is head else jnp.where(parity == 0, tail, head)
    to_b = tail if tail is head else jnp.where(parity == 0, head, tail)
    pairs = [(2 * i + 1, 2 * i + 2) for i in range(count // 2 - 1)]
    got_b = lax.ppermute(to_b, "tm", pairs + [(b, a) for a, b in pairs])
    return swap(to_a, "tm", 1), got_b


def on_device(features, weight_five, weight_six, projection, pos_weight, pos_bias, cotangent):
    members, slots = lax.axis_size("tm"), lax.axis_size("grp")
    me, slot = lax.axis_index("tm"), lax.axis_index("grp")
    where = jnp.stack([me, slot]).astype(jnp.int32)
    channels = features.shape[1]
    taps, groups, width = pos_weight.shape[0], pos_weight.shape[1], pos_weight.shape[2]
    columns = groups * width
    half = taps // 2
    own = features.shape[0] // 4
    block = own * slots

    w_taps = jnp.transpose(pos_weight, (1, 2, 3, 0))
    blocks = [features] + [swap(features, "grp", e) for e in range(1, slots)]
    five, layout = spread(jnp.transpose(weight_five, (0, 2, 1)), members)
    proj_half = lax.dynamic_slice_in_dim(projection, slot * columns, columns, 1)
    proj_half = jnp.pad(proj_half, ((0, 0), (0, channels - columns)))
    rest, _ = spread(
        jnp.concatenate([jnp.transpose(weight_six, (0, 2, 1)), proj_half[None]], 0), members
    )
    common = dict(layout=layout)
    taps_scratch = [pltpu.VMEM((2, channels, channels), BF16)]

    act_five = pl.pallas_call(
        functools.partial(five_body, count=slots, **common),
        in_specs=[SMEM_SPEC] + vmem_specs(slots + len(five)),
        out_specs=vmem_specs(1)[0],
        out_shape=jax.ShapeDtypeStruct((2 * block, channels), BF16),
        scratch_shapes=taps_scratch,
        compiler_params=PARAMS,
        name="five",
    )(where, *blocks, *five)
    normed, unit, inv_dev = pl.pallas_call(
        functools.partial(six_body, count=slots, **common),
        in_specs=[SMEM_SPEC] + vmem_specs(1 + len(rest)),
        out_specs=vmem_specs(3),
        out_shape=[
            jax.ShapeDtypeStruct((block, channels), BF16),
            jax.ShapeDtypeStruct((own, channels), F32),
            jax.ShapeDtypeStruct((own, 128), F32),
        ],
        scratch_shapes=taps_scratch,
        compiler_params=PARAMS,
        name="six",
    )(where, act_five, *rest)

    whole = block == half
    tail = normed if whole else normed[block - half :]
    head = normed if whole else normed[:half]
    got_a, got_b = halo(tail, head, me % 2)
    proj = pl.pallas_call(
        functools.partial(project_body, **common),
        in_specs=[SMEM_SPEC] + [ANY_SPEC] * len(rest),
        out_specs=vmem_specs(1)[0],
        out_shape=jax.ShapeDtypeStruct((channels, columns), BF16),
        scratch_shapes=[
            pltpu.VMEM((channels, channels), BF16),
            pltpu.SemaphoreType.DMA((members,)),
        ],
        compiler_params=PARAMS,
        name="project",
    )(where, *rest)
    conv_scratch = [
        pltpu.VMEM((groups, width, width, taps), BF16),
        pltpu.VMEM((columns, taps), F32),
        pltpu.VMEM((columns, taps), F32),
        pltpu.VMEM((groups, half, width), F32),
        pltpu.SemaphoreType.DMA((groups,)),
    ]
    encoded, slope_rev = pl.pallas_call(
        forward_body,
        in_specs=[SMEM_SPEC] + vmem_specs(4) + [ANY_SPEC] + vmem_specs(2),
        out_specs=vmem_specs(2),
        out_shape=[jax.ShapeDtypeStruct((block, columns), BF16)] * 2,
        scratch_shapes=conv_scratch,
        compiler_params=PARAMS,
        name="forward",
    )(where, normed, got_a, got_b, proj, w_taps, cotangent, pos_bias.reshape(1, columns))

    tail = slope_rev if whole else slope_rev[block - half :]
    head = slope_rev if whole else slope_rev[:half]
    got_a, got_b = halo(tail, head, me % 2)
    scale = 1.0 / math.sqrt(own * members * slots)
    share = channels // members
    finals = [0, members // 4, members // 2, 3 * (members // 4)]
    masks, mask = [], 2
    while mask < members // 4:
        masks.append(mask)
        mask *= 2
    order = finals
    for mask in reversed(masks):
        order = order + [p ^ mask for p in order]
    kept, sent, unit_grad = pl.pallas_call(
        functools.partial(backward_body, scale=scale, order=order),
        in_specs=[SMEM_SPEC] + vmem_specs(3) + [ANY_SPEC] + vmem_specs(3),
        out_specs=vmem_specs(3),
        out_shape=[jax.ShapeDtypeStruct((members // 2, share, columns), BF16)] * 2
        + [jax.ShapeDtypeStruct((slots, own, channels), F32)],
        scratch_shapes=conv_scratch
        + [
            pltpu.VMEM((width, width, taps), BF16),
            pltpu.VMEM((block, columns), BF16),
            pltpu.VMEM((members, share, columns), F32),
            pltpu.VMEM((slots, own, channels), F32),
        ],
        compiler_params=PARAMS,
        name="backward",
    )(where, slope_rev, got_a, got_b, w_taps, cotangent, normed, proj)

    total = (kept.astype(F32) + swap(sent, "tm", 1).astype(F32)).astype(BF16)
    for mask in masks:
        middle = total.shape[0] // 2
        got = swap(total[middle:], "tm", mask)
        total = (total[:middle].astype(F32) + got.astype(F32)).astype(BF16)
    parts = [swap(total[n], "tm", p) for n, p in enumerate(finals) if p]
    projection_grad = total[0].astype(F32) + sum(p.astype(F32) for p in parts)

    grad_unit = unit_grad[0]
    for e in range(1, slots):
        grad_unit = grad_unit + swap(unit_grad[e].astype(BF16), "grp", e).astype(F32)
    first_mean = jnp.mean(grad_unit, axis=-1, keepdims=True)
    second_mean = jnp.mean(grad_unit * unit, axis=-1, keepdims=True)
    feature_grad = (inv_dev[:, :1] * (grad_unit - first_mean - unit * second_mean)).astype(BF16)
    return (encoded, feature_grad, projection_grad)


def solution(mesh):
    in_specs = (
        P(("tm", "grp"), None),
        P(None, None, "tm"),
        P(None, None, "tm"),
        P("tm", None),
        P(None, "grp", None, None),
        P("grp"),
        P("tm", "grp"),
    )
    out_specs = (P("tm", "grp"), P(("tm", "grp"), None), P("tm", "grp"))

    return jax.shard_map(
        on_device, mesh=mesh, in_specs=in_specs, out_specs=out_specs, check_vma=False
    )
```

```python
import functools
import math

import jax
import jax.numpy as jnp
from jax import lax
from jax.experimental import pallas as pl
from jax.experimental.pallas import tpu as pltpu
from jax.sharding import PartitionSpec as P


EPS = 1e-05
F32 = jnp.float32
BF16 = jnp.bfloat16
VMEM_LIMIT = 56 * 1024 * 1024
SUB = 8


def dot_nn(a, b):
    return lax.dot_general(a, b, (((1,), (0,)), ((), ())), preferred_element_type=F32)


def dot_nt(a, b):
    return lax.dot_general(a, b, (((1,), (1,)), ((), ())), preferred_element_type=F32)


def normalize(v):
    average = jnp.mean(v, axis=-1, keepdims=True)
    centred = v - average
    inv_dev = lax.rsqrt(jnp.mean(centred * centred, axis=-1, keepdims=True) + EPS)
    return centred * inv_dev, inv_dev


def phi_cdf(v):
    return 0.5 * (1.0 + lax.erf(v * 0.7071067811865476))


def pick_rows(rows, first):
    r = lax.broadcasted_iota(jnp.int32, (rows, 2 * rows), 0)
    c = lax.broadcasted_iota(jnp.int32, (rows, 2 * rows), 1)
    return jnp.where(c == 2 * r + first, 1.0, 0.0).astype(BF16)


def flip_rows(rows):
    r = lax.broadcasted_iota(jnp.int32, (rows, rows), 0)
    c = lax.broadcasted_iota(jnp.int32, (rows, rows), 1)
    return jnp.where(c == rows - 1 - r, 1.0, 0.0).astype(BF16)


def place_shards(idx, layout, stacks, first, taps, full):
    for offs, ref in zip(layout, stacks):
        width = ref.shape[2]
        for q, off in enumerate(offs):
            at = pl.multiple_of((idx ^ off) * width, width)
            for tap in range(taps):
                full[tap, pl.ds(at, width), :] = ref[q, first + tap]


def strided(blocks, full):
    rows = blocks[0].shape[0] // 2
    even = [dot_nn(pick_rows(rows, 0), b).astype(BF16) for b in blocks]
    odd = [dot_nn(pick_rows(rows, 1), b).astype(BF16) for b in blocks]
    even, odd = jnp.concatenate(even, 0), jnp.concatenate(odd, 0)
    mixed = dot_nt(even, full[0]) + dot_nt(odd, full[1])
    unit, _ = normalize(mixed)
    return (unit * phi_cdf(unit)).astype(BF16)


def five_body(where, *refs, layout, count):
    blocks, stacks = refs[:count], refs[count : count + len(layout)]
    out, full = refs[count + len(layout) :]
    place_shards(where[0], layout, stacks, 0, 2, full)
    out[...] = strided([b[...] for b in blocks], full)


def six_body(where, act, *refs, layout, count):
    stacks = refs[: len(layout)]
    normed, unit_own, inv_own, full = refs[len(layout) :]
    place_shards(where[0], layout, stacks, 0, 2, full)
    rows = act.shape[0] // count
    act_six = strided([act[e * rows : (e + 1) * rows] for e in range(count)], full)
    unit, inv_dev = normalize(act_six.astype(F32))
    own = rows // 2
    for e in range(count):
        at = pl.multiple_of((where[1] ^ e) * own, own)
        normed[pl.ds(at, own), :] = unit[e * own : (e + 1) * own].astype(BF16)
    unit_own[...] = unit[:own]
    inv_own[...] = jnp.broadcast_to(inv_dev[:own], inv_own.shape)


def tap_copy(w_any, w_vmem, sems, g):
    return pltpu.make_async_copy(w_any.at[g], w_vmem.at[g], sems.at[g])


def conv_group(weights, first, wrap, rows):
    size, _, taps = weights.shape
    s = lax.broadcasted_iota(jnp.int32, (rows, taps), 0)
    j = lax.broadcasted_iota(jnp.int32, (rows, taps), 1)
    mask = j < rows - 1 - s
    total = None
    for b in range(0, size, SUB):
        parts = []
        for i in range(b, b + SUB):
            u = jnp.where(mask, wrap[i : i + 1, :], first[i : i + 1, :])
            u = pltpu.roll(u, taps - (rows - 1), 1, stride=1, stride_axis=0)
            parts.append(u.astype(BF16))
        tiles = [weights[i] for i in range(b, b + SUB)]
        term = dot_nt(jnp.concatenate(parts, 1), jnp.concatenate(tiles, 1))
        total = term if total is None else total + term
    return total


def conv(w_any, w_vmem, turned, sems, first, wrap, acc, chunk):
    groups, width = w_vmem.shape[:2]
    rows = acc.shape[1]

    def step(g, carry):
        if chunk == 0:
            tap_copy(w_any, w_vmem, sems, g).wait()

            @pl.when(g + 1 < groups)
            def _():
                tap_copy(w_any, w_vmem, sems, g + 1).start()

        weights = w_vmem.at[g]
        if turned is not None:
            turned[...] = jnp.swapaxes(w_vmem[g], 0, 1)
            weights = turned
        here = pl.ds(pl.multiple_of(g * width, 8), width)
        acc[g] = conv_group(weights, first.at[here], wrap.at[here], rows)
        return carry

    lax.fori_loop(0, groups, step, 0)
    return jnp.concatenate([acc[g] for g in range(groups)], 1)


def forward_body(where, normed, got_a, got_b, *refs, layout):
    stacks = refs[: len(layout)]
    w_any, cot, bias, encoded, slope_rev, proj, full = refs[len(layout) : len(layout) + 7]
    w_vmem, first, wrap, acc, sems = refs[len(layout) + 7 :]
    tap_copy(w_any, w_vmem, sems, 0).start()
    place_shards(where[0], layout, stacks, 0, 1, full)
    proj[...] = full[0, :, : proj.shape[1]]
    odd = where[0] % 2 == 1
    low = jnp.where(odd, got_a[...], got_b[...])
    high = jnp.where(odd, got_b[...], got_a[...])
    rows = got_a.shape[0]
    chunks = normed.shape[0] // rows
    ext = jnp.concatenate([low, normed[...], high], 0)
    hidden = dot_nn(ext, proj[...]).astype(BF16).astype(F32)
    part = lambda c: hidden[c * rows : (c + 1) * rows]
    flip = flip_rows(rows)
    for c in range(chunks):
        first[...] = jnp.concatenate([part(c), part(c + 1)], 0).T
        wrap[...] = jnp.concatenate([part(c + 2), part(c + 1)], 0).T
        pos = conv(w_any, w_vmem, None, sems, first, wrap, acc, c)
        pos = pos + bias[...].astype(F32)
        cdf = phi_cdf(pos)
        here = slice(c * rows, (c + 1) * rows)
        cot_rev = dot_nn(flip, cot[here, :])
        hid_rev = dot_nn(flip, part(c + 1).astype(BF16))
        enc_rev = (hid_rev + pos * cdf).astype(BF16)
        encoded[here, :] = dot_nn(flip, enc_rev).astype(BF16)
        slope = cdf + pos * jnp.exp(-0.5 * pos * pos) * 0.3989422804014327
        slope_rev[here, :] = (cot_rev * slope).astype(BF16)


def backward_body(where, slope_rev, got_a, got_b, w_any, cot, normed, proj, *refs, scale, order):
    kept, sent, unit_grad, unit_sent, w_vmem, first, wrap, acc, sems = refs[:9]
    turned, hid_grad, full, rows_f32 = refs[9:]
    tap_copy(w_any, w_vmem, sems, 0).start()
    odd = where[0] % 2 == 1
    low = jnp.where(odd, got_a[...], got_b[...])
    high = jnp.where(odd, got_b[...], got_a[...])
    rows = got_a.shape[0]
    chunks = slope_rev.shape[0] // rows
    ext = jnp.concatenate([low, slope_rev[...], high], 0).astype(F32)
    part = lambda c: ext[c * rows : (c + 1) * rows]
    for c in range(chunks):
        first[...] = jnp.concatenate([part(c + 2), part(c + 1)], 0).T
        wrap[...] = jnp.concatenate([part(c), part(c + 1)], 0).T
        back = conv(w_any, w_vmem, turned, sems, first, wrap, acc, c)
        here = slice(c * rows, (c + 1) * rows)
        hid_grad[here, :] = (cot[here, :].astype(F32) + back).astype(BF16)
    grad = hid_grad[...]
    full[...] = (
        dot_nn(normed[...].astype(F32).T.astype(BF16), grad) * scale
    ).reshape(full.shape)
    for n, p in enumerate(order):
        kept[n] = full[where[0] ^ p].astype(BF16)
        sent[n] = full[where[0] ^ (p ^ 1)].astype(BF16)
    slots = rows_f32.shape[0]
    rows_f32[...] = dot_nt(grad, proj[...]).reshape(rows_f32.shape)
    unit_grad[...] = rows_f32[where[1]]
    for e in range(1, slots):
        unit_sent[e - 1] = rows_f32[where[1] ^ e].astype(BF16)


def vmem_specs(count):
    return [pl.BlockSpec(memory_space=pltpu.VMEM)] * count


SMEM_SPEC = pl.BlockSpec(memory_space=pltpu.SMEM)
ANY_SPEC = pl.BlockSpec(memory_space=pl.ANY)
PARAMS = pltpu.CompilerParams(vmem_limit_bytes=VMEM_LIMIT)


def swap(values, axis, mask):
    count = lax.axis_size(axis)
    return lax.ppermute(values, axis, [(i, i ^ mask) for i in range(count)])


def spread_near(shards, count):
    offs = [0] + [n * (count // 4) for n in (1, 2, 3)]
    joined = shards[0] if len(shards) == 1 else jnp.concatenate(shards, 0)
    pieces = [joined] + [swap(joined, "tm", m) for m in offs[1:]]
    stack = jnp.stack(pieces)
    stacks, at = [], 0
    for shard in shards:
        stacks.append(stack[:, at : at + shard.shape[0]])
        at += shard.shape[0]
    return stacks, offs


def spread_far(stack, offs, count):
    stacks, layout = [stack], [offs]
    mask = count // 8
    while mask >= 1:
        got = []
        for part in stacks:
            got.append(swap(part, "tm", mask))
        stacks = stacks + got
        layout = layout + [[o ^ mask for o in offs] for offs in layout]
        mask //= 2
    return stacks, layout


def halo(tail, head, parity):
    count = lax.axis_size("tm")
    to_a = tail if tail is head else jnp.where(parity == 0, tail, head)
    to_b = tail if tail is head else jnp.where(parity == 0, head, tail)
    pairs = [(2 * i + 1, 2 * i + 2) for i in range(count // 2 - 1)]
    got_b = lax.ppermute(to_b, "tm", pairs + [(b, a) for a, b in pairs])
    return swap(to_a, "tm", 1), got_b


def on_device(features, weight_five, weight_six, projection, pos_weight, pos_bias, cotangent):
    members, slots = lax.axis_size("tm"), lax.axis_size("grp")
    me, slot = lax.axis_index("tm"), lax.axis_index("grp")
    where = jnp.stack([me, slot]).astype(jnp.int32)
    channels = features.shape[1]
    taps, groups, width = pos_weight.shape[0], pos_weight.shape[1], pos_weight.shape[2]
    columns = groups * width
    half = taps // 2
    own = features.shape[0] // 4
    block = own * slots

    w_taps = jnp.transpose(pos_weight, (1, 2, 3, 0))
    blocks = [features] + [swap(features, "grp", e) for e in range(1, slots)]
    bias = pos_bias.reshape(1, columns)
    proj_half = lax.dynamic_slice_in_dim(projection, slot * columns, columns, 1)
    proj_half = jnp.pad(proj_half, ((0, 0), (0, channels - columns)))
    (five,), offs = spread_near([jnp.transpose(weight_five, (0, 2, 1))], members)
    (six, last), _ = spread_near(
        [jnp.transpose(weight_six, (0, 2, 1)), proj_half[None]], members
    )
    five, layout = spread_far(five, offs, members)
    six, _ = spread_far(six, offs, members)
    last, _ = spread_far(last, offs, members)
    common = dict(layout=layout)
    taps_scratch = [pltpu.VMEM((2, channels, channels), BF16)]

    act_five = pl.pallas_call(
        functools.partial(five_body, count=slots, **common),
        in_specs=[SMEM_SPEC] + vmem_specs(slots + len(five)),
        out_specs=vmem_specs(1)[0],
        out_shape=jax.ShapeDtypeStruct((2 * block, channels), BF16),
        scratch_shapes=taps_scratch,
        compiler_params=PARAMS,
        name="five",
    )(where, *blocks, *five)
    normed, unit, inv_dev = pl.pallas_call(
        functools.partial(six_body, count=slots, **common),
        in_specs=[SMEM_SPEC] + vmem_specs(1 + len(six)),
        out_specs=vmem_specs(3),
        out_shape=[
            jax.ShapeDtypeStruct((block, channels), BF16),
            jax.ShapeDtypeStruct((own, channels), F32),
            jax.ShapeDtypeStruct((own, 128), F32),
        ],
        scratch_shapes=taps_scratch,
        compiler_params=PARAMS,
        name="six",
    )(where, act_five, *six)

    whole = block == half
    tail = normed if whole else normed[block - half :]
    head = normed if whole else normed[:half]
    got_a, got_b = halo(tail, head, me % 2)
    conv_scratch = [
        pltpu.VMEM((groups, width, width, taps), BF16),
        pltpu.VMEM((columns, taps), F32),
        pltpu.VMEM((columns, taps), F32),
        pltpu.VMEM((groups, half, width), F32),
        pltpu.SemaphoreType.DMA((groups,)),
    ]
    encoded, slope_rev, proj = pl.pallas_call(
        functools.partial(forward_body, **common),
        in_specs=[SMEM_SPEC] + vmem_specs(3 + len(last)) + [ANY_SPEC] + vmem_specs(2),
        out_specs=vmem_specs(3),
        out_shape=[jax.ShapeDtypeStruct((block, columns), BF16)] * 2
        + [jax.ShapeDtypeStruct((channels, columns), BF16)],
        scratch_shapes=[pltpu.VMEM((1, channels, channels), BF16)] + conv_scratch,
        compiler_params=PARAMS,
        name="forward",
    )(where, normed, got_a, got_b, *last, w_taps, cotangent, bias)

    tail = slope_rev if whole else slope_rev[block - half :]
    head = slope_rev if whole else slope_rev[:half]
    got_a, got_b = halo(tail, head, me % 2)
    scale = 1.0 / math.sqrt(own * members * slots)
    share = channels // members
    finals = [0, members // 4, members // 2, 3 * (members // 4)]
    masks, mask = [], 2
    while mask < members // 4:
        masks.append(mask)
        mask *= 2
    order = finals
    for mask in reversed(masks):
        order = order + [p ^ mask for p in order]
    kept, sent, unit_grad, unit_sent = pl.pallas_call(
        functools.partial(backward_body, scale=scale, order=order),
        in_specs=[SMEM_SPEC] + vmem_specs(3) + [ANY_SPEC] + vmem_specs(3),
        out_specs=vmem_specs(4),
        out_shape=[jax.ShapeDtypeStruct((members // 2, share, columns), BF16)] * 2
        + [
            jax.ShapeDtypeStruct((own, channels), F32),
            jax.ShapeDtypeStruct((slots - 1, own, channels), BF16),
        ],
        scratch_shapes=conv_scratch
        + [
            pltpu.VMEM((width, width, taps), BF16),
            pltpu.VMEM((block, columns), BF16),
            pltpu.VMEM((members, share, columns), F32),
            pltpu.VMEM((slots, own, channels), F32),
        ],
        compiler_params=PARAMS,
        name="backward",
    )(where, slope_rev, got_a, got_b, w_taps, cotangent, normed, proj)

    got = swap(sent, "tm", 1)
    total = (kept.astype(F32) + got.astype(F32)).astype(BF16)
    for mask in masks:
        middle = total.shape[0] // 2
        got = swap(total[middle:], "tm", mask)
        total = (total[:middle].astype(F32) + got.astype(F32)).astype(BF16)
    parts = [swap(total[n], "tm", p) for n, p in enumerate(finals) if p]
    projection_grad = total[0].astype(F32) + sum(p.astype(F32) for p in parts)

    grad_unit = unit_grad
    for e in range(1, slots):
        got = swap(unit_sent[e - 1], "grp", e)
        grad_unit = grad_unit + got.astype(F32)
    first_mean = jnp.mean(grad_unit, axis=-1, keepdims=True)
    second_mean = jnp.mean(grad_unit * unit, axis=-1, keepdims=True)
    feature_grad = (inv_dev[:, :1] * (grad_unit - first_mean - unit * second_mean)).astype(BF16)
    return (encoded, feature_grad, projection_grad)


def solution(mesh):
    in_specs = (
        P(("tm", "grp"), None),
        P(None, None, "tm"),
        P(None, None, "tm"),
        P("tm", None),
        P(None, "grp", None, None),
        P("grp"),
        P("tm", "grp"),
    )
    out_specs = (P("tm", "grp"), P(("tm", "grp"), None), P("tm", "grp"))

    return jax.shard_map(
        on_device, mesh=mesh, in_specs=in_specs, out_specs=out_specs, check_vma=False
    )
```

```python
import functools
import math

import jax
import jax.numpy as jnp
from jax import lax
from jax.experimental import pallas as pl
from jax.experimental.pallas import tpu as pltpu
from jax.sharding import PartitionSpec as P


EPS = 1e-05
F32 = jnp.float32
BF16 = jnp.bfloat16
SUB = 8
CONV_MB = 16


def dot_nn(a, b):
    return lax.dot_general(a, b, (((1,), (0,)), ((), ())), preferred_element_type=F32)


def dot_nt(a, b):
    return lax.dot_general(a, b, (((1,), (1,)), ((), ())), preferred_element_type=F32)


def normalize(v):
    average = jnp.mean(v, axis=-1, keepdims=True)
    centred = v - average
    inv_dev = lax.rsqrt(jnp.mean(centred * centred, axis=-1, keepdims=True) + EPS)
    return centred * inv_dev, inv_dev


def phi_cdf(v):
    return 0.5 * (1.0 + lax.erf(v * 0.7071067811865476))


def pick_rows(rows, first):
    r = lax.broadcasted_iota(jnp.int32, (rows, 2 * rows), 0)
    c = lax.broadcasted_iota(jnp.int32, (rows, 2 * rows), 1)
    return jnp.where(c == 2 * r + first, 1.0, 0.0).astype(BF16)


def flip_rows(rows):
    r = lax.broadcasted_iota(jnp.int32, (rows, rows), 0)
    c = lax.broadcasted_iota(jnp.int32, (rows, rows), 1)
    return jnp.where(c == rows - 1 - r, 1.0, 0.0).astype(BF16)


def place_shards(idx, layout, stacks, first, taps, full):
    for offs, ref in zip(layout, stacks):
        width = ref.shape[2]
        for q, off in enumerate(offs):
            at = pl.multiple_of((idx ^ off) * width, width)
            for tap in range(taps):
                full[tap, pl.ds(at, width), :] = ref[q, first + tap]


def strided(blocks, full):
    rows = blocks[0].shape[0] // 2
    even = [dot_nn(pick_rows(rows, 0), b).astype(BF16) for b in blocks]
    odd = [dot_nn(pick_rows(rows, 1), b).astype(BF16) for b in blocks]
    even, odd = jnp.concatenate(even, 0), jnp.concatenate(odd, 0)
    mixed = dot_nt(even, full[0]) + dot_nt(odd, full[1])
    unit, _ = normalize(mixed)
    return (unit * phi_cdf(unit)).astype(BF16)


def tap_copies(w_any, w_out, sems, start):
    count = sems.shape[1]
    size = w_out.shape[1] // count
    copies = []
    for g in range(w_out.shape[0]):
        for c in range(count):
            part = pl.ds(c * size, size)
            copies.append(
                pltpu.make_async_copy(
                    w_any.at[start + g, part], w_out.at[g, part], sems.at[g, c]
                )
            )
    for copy in copies:
        copy.start()
    return copies


def five_body(where, *refs, layout, count):
    blocks, stacks = refs[:count], refs[count : count + len(layout)]
    w_any, out, w_out, full, sems = refs[count + len(layout) :]
    copies = tap_copies(w_any, w_out, sems, 0)
    place_shards(where[0], layout, stacks, 0, 2, full)
    out[...] = strided([b[...] for b in blocks], full)
    for copy in copies:
        copy.wait()


def six_body(where, act, *refs, layout, count, start):
    stacks = refs[: len(layout)]
    if start is None:
        normed, unit_own, inv_own, full = refs[len(layout) :]
        copies = []
    else:
        w_any, normed, unit_own, inv_own, w_out, full, sems = refs[len(layout) :]
        copies = tap_copies(w_any, w_out, sems, start)
    place_shards(where[0], layout, stacks, 0, 2, full)
    rows = act.shape[0] // count
    act_six = strided([act[e * rows : (e + 1) * rows] for e in range(count)], full)
    unit, inv_dev = normalize(act_six.astype(F32))
    own = rows // 2
    for e in range(count):
        at = pl.multiple_of((where[1] ^ e) * own, own)
        normed[pl.ds(at, own), :] = unit[e * own : (e + 1) * own].astype(BF16)
    unit_own[...] = unit[:own]
    inv_own[...] = jnp.broadcast_to(inv_dev[:own], inv_own.shape)
    for copy in copies:
        copy.wait()


def conv_group(weights, first, wrap, rows):
    size, _, taps = weights.shape
    s = lax.broadcasted_iota(jnp.int32, (rows, taps), 0)
    j = lax.broadcasted_iota(jnp.int32, (rows, taps), 1)
    mask = j < rows - 1 - s
    total = None
    for b in range(0, size, SUB):
        parts = []
        for i in range(b, b + SUB):
            u = jnp.where(mask, wrap[i : i + 1, :], first[i : i + 1, :])
            u = pltpu.roll(u, taps - (rows - 1), 1, stride=1, stride_axis=0)
            parts.append(u.astype(BF16))
        tiles = [weights[i] for i in range(b, b + SUB)]
        term = dot_nt(jnp.concatenate(parts, 1), jnp.concatenate(tiles, 1))
        total = term if total is None else total + term
    return total


def conv(weights, turned, first, wrap, acc):
    rows, width = acc.shape[1:]
    start = 0
    for held in weights:
        def step(g, carry):
            group = held.at[g]
            if turned is not None:
                turned[...] = jnp.swapaxes(held[g], 0, 1)
                group = turned
            here = pl.ds(pl.multiple_of((start + g) * width, 8), width)
            acc[start + g] = conv_group(group, first.at[here], wrap.at[here], rows)
            return carry

        lax.fori_loop(0, held.shape[0], step, 0)
        start += held.shape[0]
    return jnp.concatenate([acc[g] for g in range(acc.shape[0])], 1)


def forward_body(where, normed, got_a, got_b, *refs, layout, held):
    stacks, refs = refs[: len(layout)], refs[len(layout) :]
    weights, refs = refs[:held], refs[held:]
    cot, bias, encoded, slope_rev, proj, full = refs[:6]
    first, wrap, acc = refs[6:]
    place_shards(where[0], layout, stacks, 0, 1, full)
    proj[...] = full[0, :, : proj.shape[1]]
    odd = where[0] % 2 == 1
    low = jnp.where(odd, got_a[...], got_b[...])
    high = jnp.where(odd, got_b[...], got_a[...])
    rows = got_a.shape[0]
    chunks = normed.shape[0] // rows
    ext = jnp.concatenate([low, normed[...], high], 0)
    hidden = dot_nn(ext, proj[...]).astype(BF16).astype(F32)
    part = lambda c: hidden[c * rows : (c + 1) * rows]
    flip = flip_rows(rows)
    for c in range(chunks):
        first[...] = jnp.concatenate([part(c), part(c + 1)], 0).T
        wrap[...] = jnp.concatenate([part(c + 2), part(c + 1)], 0).T
        pos = conv(weights, None, first, wrap, acc)
        pos = pos + bias[...].astype(F32)
        cdf = phi_cdf(pos)
        here = slice(c * rows, (c + 1) * rows)
        cot_rev = dot_nn(flip, cot[here, :])
        hid_rev = dot_nn(flip, part(c + 1).astype(BF16))
        enc_rev = (hid_rev + pos * cdf).astype(BF16)
        encoded[here, :] = dot_nn(flip, enc_rev).astype(BF16)
        slope = cdf + pos * jnp.exp(-0.5 * pos * pos) * 0.3989422804014327
        slope_rev[here, :] = (cot_rev * slope).astype(BF16)


def backward_body(where, slope_rev, got_a, got_b, *refs, scale, order, held):
    weights, refs = refs[:held], refs[held:]
    (cot, normed, proj), refs = refs[:3], refs[3:]
    kept, sent, unit_grad, unit_sent, first, wrap, acc = refs[:7]
    turned, hid_grad, full, rows_f32 = refs[7:]
    odd = where[0] % 2 == 1
    low = jnp.where(odd, got_a[...], got_b[...])
    high = jnp.where(odd, got_b[...], got_a[...])
    rows = got_a.shape[0]
    chunks = slope_rev.shape[0] // rows
    ext = jnp.concatenate([low, slope_rev[...], high], 0).astype(F32)
    part = lambda c: ext[c * rows : (c + 1) * rows]
    for c in range(chunks):
        first[...] = jnp.concatenate([part(c + 2), part(c + 1)], 0).T
        wrap[...] = jnp.concatenate([part(c), part(c + 1)], 0).T
        back = conv(weights, turned, first, wrap, acc)
        here = slice(c * rows, (c + 1) * rows)
        hid_grad[here, :] = (cot[here, :].astype(F32) + back).astype(BF16)
    grad = hid_grad[...]
    full[...] = (
        dot_nn(normed[...].astype(F32).T.astype(BF16), grad) * scale
    ).reshape(full.shape)
    for n, p in enumerate(order):
        kept[n] = full[where[0] ^ p].astype(BF16)
        sent[n] = full[where[0] ^ (p ^ 1)].astype(BF16)
    slots = rows_f32.shape[0]
    rows_f32[...] = dot_nt(grad, proj[...]).reshape(rows_f32.shape)
    unit_grad[...] = rows_f32[where[1]]
    for e in range(1, slots):
        unit_sent[e - 1] = rows_f32[where[1] ^ e].astype(BF16)


def on_chip(values):
    return [pltpu.with_memory_space_constraint(v, pltpu.VMEM) for v in values]


def vmem_specs(count):
    return [pl.BlockSpec(memory_space=pltpu.VMEM)] * count


SMEM_SPEC = pl.BlockSpec(memory_space=pltpu.SMEM)
HBM_SPEC = pl.BlockSpec(memory_space=pltpu.HBM)
PARAMS = pltpu.CompilerParams(vmem_limit_bytes=16 * 1024 * 1024)
CONV_PARAMS = pltpu.CompilerParams(vmem_limit_bytes=CONV_MB * 1024 * 1024)


def swap(values, axis, mask):
    count = lax.axis_size(axis)
    return lax.ppermute(values, axis, [(i, i ^ mask) for i in range(count)])


def spread_near(shards, count):
    offs = [0] + [n * (count // 4) for n in (1, 2, 3)]
    joined = shards[0] if len(shards) == 1 else jnp.concatenate(shards, 0)
    pieces = [joined] + [swap(joined, "tm", m) for m in offs[1:]]
    stack = jnp.stack(pieces)
    stacks, at = [], 0
    for shard in shards:
        stacks.append(stack[:, at : at + shard.shape[0]])
        at += shard.shape[0]
    return stacks, offs


def spread_far(stack, offs, count):
    stacks, layout = [stack], [offs]
    mask = count // 8
    while mask >= 1:
        got = []
        for part in stacks:
            got.append(swap(part, "tm", mask))
        stacks = stacks + got
        layout = layout + [[o ^ mask for o in offs] for offs in layout]
        mask //= 2
    return stacks, layout


def halo(tail, head, parity):
    count = lax.axis_size("tm")
    to_a = tail if tail is head else jnp.where(parity == 0, tail, head)
    to_b = tail if tail is head else jnp.where(parity == 0, head, tail)
    pairs = [(2 * i + 1, 2 * i + 2) for i in range(count // 2 - 1)]
    got_b = lax.ppermute(to_b, "tm", pairs + [(b, a) for a, b in pairs])
    return swap(to_a, "tm", 1), got_b


def on_device(features, weight_five, weight_six, projection, pos_weight, pos_bias, cotangent):
    members, slots = lax.axis_size("tm"), lax.axis_size("grp")
    me, slot = lax.axis_index("tm"), lax.axis_index("grp")
    where = jnp.stack([me, slot]).astype(jnp.int32)
    channels = features.shape[1]
    taps, groups, width = pos_weight.shape[0], pos_weight.shape[1], pos_weight.shape[2]
    columns = groups * width
    half = taps // 2
    own = features.shape[0] // 4
    block = own * slots

    w_taps = pltpu.with_memory_space_constraint(
        jnp.transpose(pos_weight, (1, 2, 3, 0)), pltpu.HBM
    )
    blocks = [features] + [swap(features, "grp", e) for e in range(1, slots)]
    bias = pos_bias.reshape(1, columns)
    proj_half = lax.dynamic_slice_in_dim(projection, slot * columns, columns, 1)
    proj_half = jnp.pad(proj_half, ((0, 0), (0, channels - columns)))
    (five,), offs = spread_near([jnp.transpose(weight_five, (0, 2, 1))], members)
    (six, last), _ = spread_near(
        [jnp.transpose(weight_six, (0, 2, 1)), proj_half[None]], members
    )
    five, layout = spread_far(five, offs, members)
    six, _ = spread_far(six, offs, members)
    last, _ = spread_far(last, offs, members)
    common = dict(layout=layout)
    taps_scratch = [pltpu.VMEM((2, channels, channels), BF16)]

    cut = (groups + 1) // 2
    tap_sems = lambda count: pltpu.SemaphoreType.DMA((count, 5))
    act_five, w_low = pl.pallas_call(
        functools.partial(five_body, count=slots, **common),
        in_specs=[SMEM_SPEC] + vmem_specs(slots + len(five)) + [HBM_SPEC],
        out_specs=vmem_specs(2),
        out_shape=[
            pltpu.VMEM((2 * block, channels), BF16),
            pltpu.VMEM((cut, width, width, taps), BF16),
        ],
        scratch_shapes=taps_scratch + [tap_sems(cut)],
        compiler_params=PARAMS,
        name="five",
    )(where, blocks[0], *on_chip(blocks[1:] + five), w_taps)
    rest = groups - cut
    results = pl.pallas_call(
        functools.partial(six_body, count=slots, start=cut if rest else None, **common),
        in_specs=[SMEM_SPEC] + vmem_specs(1 + len(six)) + ([HBM_SPEC] if rest else []),
        out_specs=vmem_specs(4 if rest else 3),
        out_shape=[
            pltpu.VMEM((block, channels), BF16),
            pltpu.VMEM((own, channels), F32),
            pltpu.VMEM((own, 128), F32),
        ]
        + ([pltpu.VMEM((rest, width, width, taps), BF16)] if rest else []),
        scratch_shapes=taps_scratch + ([tap_sems(rest)] if rest else []),
        compiler_params=PARAMS,
        name="six",
    )(where, act_five, *on_chip(six), *([w_taps] if rest else []))
    normed, unit, inv_dev = results[:3]
    weights = [w_low] + list(results[3:])

    whole = block == half
    tail = normed if whole else normed[block - half :]
    head = normed if whole else normed[:half]
    got_a, got_b = halo(tail, head, me % 2)
    conv_scratch = [
        pltpu.VMEM((columns, taps), F32),
        pltpu.VMEM((columns, taps), F32),
        pltpu.VMEM((groups, half, width), F32),
    ]
    encoded, slope_rev, proj = pl.pallas_call(
        functools.partial(forward_body, held=len(weights), **common),
        in_specs=[SMEM_SPEC] + vmem_specs(3 + len(last) + len(weights) + 2),
        out_specs=vmem_specs(3),
        out_shape=[
            jax.ShapeDtypeStruct((block, columns), BF16),
            pltpu.VMEM((block, columns), BF16),
            pltpu.VMEM((channels, columns), BF16),
        ],
        scratch_shapes=[pltpu.VMEM((1, channels, channels), BF16)] + conv_scratch,
        compiler_params=CONV_PARAMS,
        name="forward",
    )(where, normed, *on_chip([got_a, got_b] + last), *weights, cotangent, bias)

    tail = slope_rev if whole else slope_rev[block - half :]
    head = slope_rev if whole else slope_rev[:half]
    got_a, got_b = halo(tail, head, me % 2)
    scale = 1.0 / math.sqrt(own * members * slots)
    share = channels // members
    finals = [0, members // 4, members // 2, 3 * (members // 4)]
    masks, mask = [], 2
    while mask < members // 4:
        masks.append(mask)
        mask *= 2
    order = finals
    for mask in reversed(masks):
        order = order + [p ^ mask for p in order]
    kept, sent, unit_grad, unit_sent = pl.pallas_call(
        functools.partial(backward_body, scale=scale, order=order, held=len(weights)),
        in_specs=[SMEM_SPEC] + vmem_specs(6 + len(weights)),
        out_specs=vmem_specs(4),
        out_shape=[pltpu.VMEM((members // 2, share, columns), BF16)] * 2
        + [
            pltpu.VMEM((own, channels), F32),
            pltpu.VMEM((slots - 1, own, channels), BF16),
        ],
        scratch_shapes=conv_scratch
        + [
            pltpu.VMEM((width, width, taps), BF16),
            pltpu.VMEM((block, columns), BF16),
            pltpu.VMEM((members, share, columns), F32),
            pltpu.VMEM((slots, own, channels), F32),
        ],
        compiler_params=CONV_PARAMS,
        name="backward",
    )(where, slope_rev, *on_chip([got_a, got_b]), *weights, cotangent, normed, proj)

    got = swap(sent, "tm", 1)
    total = (kept.astype(F32) + got.astype(F32)).astype(BF16)
    for mask in masks:
        middle = total.shape[0] // 2
        got = swap(total[middle:], "tm", mask)
        total = (total[:middle].astype(F32) + got.astype(F32)).astype(BF16)
    parts = [swap(total[n], "tm", p) for n, p in enumerate(finals) if p]
    projection_grad = total[0].astype(F32) + sum(p.astype(F32) for p in parts)

    grad_unit = unit_grad
    for e in range(1, slots):
        got = swap(unit_sent[e - 1], "grp", e)
        grad_unit = grad_unit + got.astype(F32)
    first_mean = jnp.mean(grad_unit, axis=-1, keepdims=True)
    second_mean = jnp.mean(grad_unit * unit, axis=-1, keepdims=True)
    feature_grad = (inv_dev[:, :1] * (grad_unit - first_mean - unit * second_mean)).astype(BF16)
    return (encoded, feature_grad, projection_grad)


def solution(mesh):
    in_specs = (
        P(("tm", "grp"), None),
        P(None, None, "tm"),
        P(None, None, "tm"),
        P("tm", None),
        P(None, "grp", None, None),
        P("grp"),
        P("tm", "grp"),
    )
    out_specs = (P("tm", "grp"), P(("tm", "grp"), None), P("tm", "grp"))

    return jax.shard_map(
        on_device, mesh=mesh, in_specs=in_specs, out_specs=out_specs, check_vma=False
    )
```

```python
import functools
import math

import jax
import jax.numpy as jnp
from jax import lax
from jax.experimental import pallas as pl
from jax.experimental.pallas import tpu as pltpu
from jax.sharding import PartitionSpec as P


EPS = 1e-05
F32 = jnp.float32
BF16 = jnp.bfloat16
SUB = 8
CONV_MB = 16


def dot_nn(a, b):
    return lax.dot_general(a, b, (((1,), (0,)), ((), ())), preferred_element_type=F32)


def dot_nt(a, b):
    return lax.dot_general(a, b, (((1,), (1,)), ((), ())), preferred_element_type=F32)


def normalize(v):
    average = jnp.mean(v, axis=-1, keepdims=True)
    centred = v - average
    inv_dev = lax.rsqrt(jnp.mean(centred * centred, axis=-1, keepdims=True) + EPS)
    return centred * inv_dev, inv_dev


def phi_cdf(v):
    return 0.5 * (1.0 + lax.erf(v * 0.7071067811865476))


def pick_rows(rows, first):
    r = lax.broadcasted_iota(jnp.int32, (rows, 2 * rows), 0)
    c = lax.broadcasted_iota(jnp.int32, (rows, 2 * rows), 1)
    return jnp.where(c == 2 * r + first, 1.0, 0.0).astype(BF16)


def flip_rows(rows):
    r = lax.broadcasted_iota(jnp.int32, (rows, rows), 0)
    c = lax.broadcasted_iota(jnp.int32, (rows, rows), 1)
    return jnp.where(c == rows - 1 - r, 1.0, 0.0).astype(BF16)


def place_shards(idx, layout, stacks, first, taps, full):
    for offs, ref in zip(layout, stacks):
        width = ref.shape[2]
        for q, off in enumerate(offs):
            at = pl.multiple_of((idx ^ off) * width, width)
            for tap in range(taps):
                full[tap, pl.ds(at, width), :] = ref[q, first + tap]


def strided(blocks, full):
    rows = blocks[0].shape[0] // 2
    even = [dot_nn(pick_rows(rows, 0), b).astype(BF16) for b in blocks]
    odd = [dot_nn(pick_rows(rows, 1), b).astype(BF16) for b in blocks]
    even, odd = jnp.concatenate(even, 0), jnp.concatenate(odd, 0)
    mixed = dot_nt(even, full[0]) + dot_nt(odd, full[1])
    unit, _ = normalize(mixed)
    return (unit * phi_cdf(unit)).astype(BF16)


def tap_copies(w_any, w_out, sems, start):
    count = sems.shape[1]
    size = w_out.shape[1] // count
    copies = []
    for g in range(w_out.shape[0]):
        for c in range(count):
            part = pl.ds(c * size, size)
            copies.append(
                pltpu.make_async_copy(
                    w_any.at[start + g, part], w_out.at[g, part], sems.at[g, c]
                )
            )
    for copy in copies:
        copy.start()
    return copies


def five_body(where, *refs, layout, count):
    blocks, stacks = refs[:count], refs[count : count + len(layout)]
    w_any, out, w_out, full, sems, mine, mine_sem = refs[count + len(layout) :]
    own = pltpu.make_async_copy(blocks[0], mine, mine_sem)
    own.start()
    copies = tap_copies(w_any, w_out, sems, 0)
    place_shards(where[0], layout, stacks, 0, 2, full)
    own.wait()
    out[...] = strided([mine[...]] + [b[...] for b in blocks[1:]], full)
    for copy in copies:
        copy.wait()


def six_body(where, act, *refs, layout, count, start):
    stacks = refs[: len(layout)]
    if start is None:
        normed, unit_own, inv_own, full = refs[len(layout) :]
        copies = []
    else:
        w_any, normed, unit_own, inv_own, w_out, full, sems = refs[len(layout) :]
        copies = tap_copies(w_any, w_out, sems, start)
    place_shards(where[0], layout, stacks, 0, 2, full)
    rows = act.shape[0] // count
    act_six = strided([act[e * rows : (e + 1) * rows] for e in range(count)], full)
    unit, inv_dev = normalize(act_six.astype(F32))
    own = rows // 2
    for e in range(count):
        at = pl.multiple_of((where[1] ^ e) * own, own)
        normed[pl.ds(at, own), :] = unit[e * own : (e + 1) * own].astype(BF16)
    unit_own[...] = unit[:own]
    inv_own[...] = jnp.broadcast_to(inv_dev[:own], inv_own.shape)
    for copy in copies:
        copy.wait()


def conv_group(weights, first, wrap, rows):
    size, _, taps = weights.shape
    s = lax.broadcasted_iota(jnp.int32, (rows, taps), 0)
    j = lax.broadcasted_iota(jnp.int32, (rows, taps), 1)
    mask = j < rows - 1 - s
    total = None
    for b in range(0, size, SUB):
        parts = []
        for i in range(b, b + SUB):
            u = jnp.where(mask, wrap[i : i + 1, :], first[i : i + 1, :])
            u = pltpu.roll(u, taps - (rows - 1), 1, stride=1, stride_axis=0)
            parts.append(u.astype(BF16))
        tiles = [weights[i] for i in range(b, b + SUB)]
        term = dot_nt(jnp.concatenate(parts, 1), jnp.concatenate(tiles, 1))
        total = term if total is None else total + term
    return total


def conv(weights, turned, first, wrap, acc):
    rows, width = acc.shape[1:]
    start = 0
    for held in weights:
        def step(g, carry):
            group = held.at[g]
            if turned is not None:
                turned[...] = jnp.swapaxes(held[g], 0, 1)
                group = turned
            here = pl.ds(pl.multiple_of((start + g) * width, 8), width)
            acc[start + g] = conv_group(group, first.at[here], wrap.at[here], rows)
            return carry

        lax.fori_loop(0, held.shape[0], step, 0)
        start += held.shape[0]
    return jnp.concatenate([acc[g] for g in range(acc.shape[0])], 1)


def forward_body(where, normed, got_a, got_b, *refs, layout, held):
    stacks, refs = refs[: len(layout)], refs[len(layout) :]
    weights, refs = refs[:held], refs[held:]
    cot, bias, encoded, slope_rev, proj, full = refs[:6]
    first, wrap, acc = refs[6:]
    place_shards(where[0], layout, stacks, 0, 1, full)
    proj[...] = full[0, :, : proj.shape[1]]
    odd = where[0] % 2 == 1
    low = jnp.where(odd, got_a[...], got_b[...])
    high = jnp.where(odd, got_b[...], got_a[...])
    rows = got_a.shape[0]
    chunks = normed.shape[0] // rows
    ext = jnp.concatenate([low, normed[...], high], 0)
    hidden = dot_nn(ext, proj[...]).astype(BF16).astype(F32)
    part = lambda c: hidden[c * rows : (c + 1) * rows]
    flip = flip_rows(rows)
    for c in range(chunks):
        first[...] = jnp.concatenate([part(c), part(c + 1)], 0).T
        wrap[...] = jnp.concatenate([part(c + 2), part(c + 1)], 0).T
        pos = conv(weights, None, first, wrap, acc)
        pos = pos + bias[...].astype(F32)
        cdf = phi_cdf(pos)
        here = slice(c * rows, (c + 1) * rows)
        cot_rev = dot_nn(flip, cot[here, :])
        hid_rev = dot_nn(flip, part(c + 1).astype(BF16))
        enc_rev = (hid_rev + pos * cdf).astype(BF16)
        encoded[here, :] = dot_nn(flip, enc_rev).astype(BF16)
        slope = cdf + pos * jnp.exp(-0.5 * pos * pos) * 0.3989422804014327
        slope_rev[here, :] = (cot_rev * slope).astype(BF16)


def backward_body(where, slope_rev, got_a, got_b, *refs, scale, order, held):
    weights, refs = refs[:held], refs[held:]
    (cot, normed, proj), refs = refs[:3], refs[3:]
    kept, sent, unit_grad, unit_sent, first, wrap, acc = refs[:7]
    turned, hid_grad, full, rows_f32 = refs[7:]
    odd = where[0] % 2 == 1
    low = jnp.where(odd, got_a[...], got_b[...])
    high = jnp.where(odd, got_b[...], got_a[...])
    rows = got_a.shape[0]
    chunks = slope_rev.shape[0] // rows
    ext = jnp.concatenate([low, slope_rev[...], high], 0).astype(F32)
    part = lambda c: ext[c * rows : (c + 1) * rows]
    for c in range(chunks):
        first[...] = jnp.concatenate([part(c + 2), part(c + 1)], 0).T
        wrap[...] = jnp.concatenate([part(c), part(c + 1)], 0).T
        back = conv(weights, turned, first, wrap, acc)
        here = slice(c * rows, (c + 1) * rows)
        hid_grad[here, :] = (cot[here, :].astype(F32) + back).astype(BF16)
    grad = hid_grad[...]
    full[...] = (
        dot_nn(normed[...].astype(F32).T.astype(BF16), grad) * scale
    ).reshape(full.shape)
    for n, p in enumerate(order):
        kept[n] = full[where[0] ^ p].astype(BF16)
        sent[n] = full[where[0] ^ (p ^ 1)].astype(BF16)
    slots = rows_f32.shape[0]
    rows_f32[...] = dot_nt(grad, proj[...]).reshape(rows_f32.shape)
    unit_grad[...] = rows_f32[where[1]]
    for e in range(1, slots):
        unit_sent[e - 1] = rows_f32[where[1] ^ e].astype(BF16)


def on_chip(values):
    return [pltpu.with_memory_space_constraint(v, pltpu.VMEM) for v in values]


def in_hbm(value):
    return pltpu.with_memory_space_constraint(value, pltpu.HBM)


def vmem_specs(count):
    return [pl.BlockSpec(memory_space=pltpu.VMEM)] * count


SMEM_SPEC = pl.BlockSpec(memory_space=pltpu.SMEM)
HBM_SPEC = pl.BlockSpec(memory_space=pltpu.HBM)
PARAMS = pltpu.CompilerParams(vmem_limit_bytes=16 * 1024 * 1024)
CONV_PARAMS = pltpu.CompilerParams(vmem_limit_bytes=CONV_MB * 1024 * 1024)


def swap(values, axis, mask):
    count = lax.axis_size(axis)
    return lax.ppermute(values, axis, [(i, i ^ mask) for i in range(count)])


def spread_near(shard, count):
    offs = [n * (count // 4) for n in range(4)]
    pieces = [shard]
    for n in (1, 2, 3):
        pieces.append(swap(shard, "tm", offs[n]))
    return jnp.stack(pieces), offs


def spread_far(stack, offs, count):
    stacks, layout = [stack], [offs]
    mask = count // 8
    while mask >= 1:
        got = []
        for part in stacks:
            got.append(swap(part, "tm", mask))
        stacks = stacks + got
        layout = layout + [[o ^ mask for o in offs] for offs in layout]
        mask //= 2
    return stacks, layout


def halo(tail, head, parity):
    count = lax.axis_size("tm")
    to_a = tail if tail is head else jnp.where(parity == 0, tail, head)
    to_b = tail if tail is head else jnp.where(parity == 0, head, tail)
    pairs = [(2 * i + 1, 2 * i + 2) for i in range(count // 2 - 1)]
    got_b = lax.ppermute(to_b, "tm", pairs + [(b, a) for a, b in pairs])
    return swap(to_a, "tm", 1), got_b


def on_device(features, weight_five, weight_six, projection, pos_weight, pos_bias, cotangent):
    members, slots = lax.axis_size("tm"), lax.axis_size("grp")
    me, slot = lax.axis_index("tm"), lax.axis_index("grp")
    where = jnp.stack([me, slot]).astype(jnp.int32)
    channels = features.shape[1]
    taps, groups, width = pos_weight.shape[0], pos_weight.shape[1], pos_weight.shape[2]
    columns = groups * width
    half = taps // 2
    own = features.shape[0] // 4
    block = own * slots

    w_taps = in_hbm(jnp.transpose(pos_weight, (1, 2, 3, 0)))
    blocks = [features] + [swap(features, "grp", e) for e in range(1, slots)]
    bias = pos_bias.reshape(1, columns)
    proj_half = lax.dynamic_slice_in_dim(projection, slot * columns, columns, 1)
    proj_half = jnp.pad(proj_half, ((0, 0), (0, channels - columns)))
    five, offs = spread_near(jnp.transpose(weight_five, (0, 2, 1)), members)
    six, _ = spread_near(jnp.transpose(weight_six, (0, 2, 1)), members)
    last, _ = spread_near(proj_half[None], members)
    five, layout = spread_far(five, offs, members)
    six, _ = spread_far(six, offs, members)
    last, _ = spread_far(last, offs, members)
    common = dict(layout=layout)
    taps_scratch = [pltpu.VMEM((2, channels, channels), BF16)]

    cut = (groups + 1) // 2
    tap_sems = lambda count: pltpu.SemaphoreType.DMA((count, 5))
    act_five, w_low = pl.pallas_call(
        functools.partial(five_body, count=slots, **common),
        in_specs=[SMEM_SPEC, HBM_SPEC] + vmem_specs(slots - 1 + len(five)) + [HBM_SPEC],
        out_specs=vmem_specs(2),
        out_shape=[
            pltpu.VMEM((2 * block, channels), BF16),
            pltpu.VMEM((cut, width, width, taps), BF16),
        ],
        scratch_shapes=taps_scratch
        + [tap_sems(cut), pltpu.VMEM(features.shape, BF16), pltpu.SemaphoreType.DMA(())],
        compiler_params=PARAMS,
        name="five",
    )(where, in_hbm(blocks[0]), *on_chip(blocks[1:] + five), w_taps)
    rest = groups - cut
    results = pl.pallas_call(
        functools.partial(six_body, count=slots, start=cut if rest else None, **common),
        in_specs=[SMEM_SPEC] + vmem_specs(1 + len(six)) + ([HBM_SPEC] if rest else []),
        out_specs=vmem_specs(4 if rest else 3),
        out_shape=[
            pltpu.VMEM((block, channels), BF16),
            pltpu.VMEM((own, channels), F32),
            pltpu.VMEM((own, 128), F32),
        ]
        + ([pltpu.VMEM((rest, width, width, taps), BF16)] if rest else []),
        scratch_shapes=taps_scratch + ([tap_sems(rest)] if rest else []),
        compiler_params=PARAMS,
        name="six",
    )(where, act_five, *on_chip(six), *([w_taps] if rest else []))
    normed, unit, inv_dev = results[:3]
    weights = [w_low] + list(results[3:])

    whole = block == half
    tail = normed if whole else normed[block - half :]
    head = normed if whole else normed[:half]
    got_a, got_b = halo(tail, head, me % 2)
    conv_scratch = [
        pltpu.VMEM((columns, taps), F32),
        pltpu.VMEM((columns, taps), F32),
        pltpu.VMEM((groups, half, width), F32),
    ]
    encoded, slope_rev, proj = pl.pallas_call(
        functools.partial(forward_body, held=len(weights), **common),
        in_specs=[SMEM_SPEC] + vmem_specs(3 + len(last) + len(weights) + 2),
        out_specs=vmem_specs(3),
        out_shape=[
            jax.ShapeDtypeStruct((block, columns), BF16),
            pltpu.VMEM((block, columns), BF16),
            pltpu.VMEM((channels, columns), BF16),
        ],
        scratch_shapes=[pltpu.VMEM((1, channels, channels), BF16)] + conv_scratch,
        compiler_params=CONV_PARAMS,
        name="forward",
    )(where, normed, *on_chip([got_a, got_b] + last), *weights, cotangent, bias)

    tail = slope_rev if whole else slope_rev[block - half :]
    head = slope_rev if whole else slope_rev[:half]
    got_a, got_b = halo(tail, head, me % 2)
    scale = 1.0 / math.sqrt(own * members * slots)
    share = channels // members
    finals = [0, members // 4, members // 2, 3 * (members // 4)]
    masks, mask = [], 2
    while mask < members // 4:
        masks.append(mask)
        mask *= 2
    order = finals
    for mask in reversed(masks):
        order = order + [p ^ mask for p in order]
    kept, sent, unit_grad, unit_sent = pl.pallas_call(
        functools.partial(backward_body, scale=scale, order=order, held=len(weights)),
        in_specs=[SMEM_SPEC] + vmem_specs(6 + len(weights)),
        out_specs=vmem_specs(4),
        out_shape=[pltpu.VMEM((members // 2, share, columns), BF16)] * 2
        + [
            pltpu.VMEM((own, channels), F32),
            pltpu.VMEM((slots - 1, own, channels), BF16),
        ],
        scratch_shapes=conv_scratch
        + [
            pltpu.VMEM((width, width, taps), BF16),
            pltpu.VMEM((block, columns), BF16),
            pltpu.VMEM((members, share, columns), F32),
            pltpu.VMEM((slots, own, channels), F32),
        ],
        compiler_params=CONV_PARAMS,
        name="backward",
    )(where, slope_rev, *on_chip([got_a, got_b]), *weights, cotangent, normed, proj)

    got = swap(sent, "tm", 1)
    total = (kept.astype(F32) + got.astype(F32)).astype(BF16)
    for mask in masks:
        middle = total.shape[0] // 2
        got = swap(total[middle:], "tm", mask)
        total = (total[:middle].astype(F32) + got.astype(F32)).astype(BF16)
    parts = []
    for n in (1, 2, 3):
        parts.append(swap(total[n], "tm", finals[n]))
    projection_grad = total[0].astype(F32) + sum(p.astype(F32) for p in parts)

    grad_unit = unit_grad
    for e in range(1, slots):
        got = swap(unit_sent[e - 1], "grp", e)
        grad_unit = grad_unit + got.astype(F32)
    first_mean = jnp.mean(grad_unit, axis=-1, keepdims=True)
    second_mean = jnp.mean(grad_unit * unit, axis=-1, keepdims=True)
    feature_grad = (inv_dev[:, :1] * (grad_unit - first_mean - unit * second_mean)).astype(BF16)
    return (encoded, feature_grad, projection_grad)


def solution(mesh):
    in_specs = (
        P(("tm", "grp"), None),
        P(None, None, "tm"),
        P(None, None, "tm"),
        P("tm", None),
        P(None, "grp", None, None),
        P("grp"),
        P("tm", "grp"),
    )
    out_specs = (P("tm", "grp"), P(("tm", "grp"), None), P("tm", "grp"))

    return jax.shard_map(
        on_device, mesh=mesh, in_specs=in_specs, out_specs=out_specs, check_vma=False
    )
```

```python
import functools
import math

import jax
import jax.numpy as jnp
from jax import lax
from jax.experimental import pallas as pl
from jax.experimental.pallas import tpu as pltpu
from jax.sharding import PartitionSpec as P


EPS = 1e-05
F32 = jnp.float32
BF16 = jnp.bfloat16
SUB = 8
CONV_MB = 16


def dot_nn(a, b):
    return lax.dot_general(a, b, (((1,), (0,)), ((), ())), preferred_element_type=F32)


def dot_nt(a, b):
    return lax.dot_general(a, b, (((1,), (1,)), ((), ())), preferred_element_type=F32)


def normalize(v):
    average = jnp.mean(v, axis=-1, keepdims=True)
    centred = v - average
    inv_dev = lax.rsqrt(jnp.mean(centred * centred, axis=-1, keepdims=True) + EPS)
    return centred * inv_dev, inv_dev


def phi_cdf(v):
    return 0.5 * (1.0 + lax.erf(v * 0.7071067811865476))


def pick_rows(rows, first):
    r = lax.broadcasted_iota(jnp.int32, (rows, 2 * rows), 0)
    c = lax.broadcasted_iota(jnp.int32, (rows, 2 * rows), 1)
    return jnp.where(c == 2 * r + first, 1.0, 0.0).astype(BF16)


def flip_rows(rows):
    r = lax.broadcasted_iota(jnp.int32, (rows, rows), 0)
    c = lax.broadcasted_iota(jnp.int32, (rows, rows), 1)
    return jnp.where(c == rows - 1 - r, 1.0, 0.0).astype(BF16)


def place_shards(idx, layout, stacks, first, taps, full):
    for offs, ref in zip(layout, stacks):
        width = ref.shape[2]
        for q, off in enumerate(offs):
            at = pl.multiple_of((idx ^ off) * width, width)
            for tap in range(taps):
                full[tap, pl.ds(at, width), :] = ref[q, first + tap]


def strided(blocks, full):
    rows = blocks[0].shape[0] // 2
    even = [dot_nn(pick_rows(rows, 0), b).astype(BF16) for b in blocks]
    odd = [dot_nn(pick_rows(rows, 1), b).astype(BF16) for b in blocks]
    even, odd = jnp.concatenate(even, 0), jnp.concatenate(odd, 0)
    mixed = dot_nt(even, full[0]) + dot_nt(odd, full[1])
    unit, _ = normalize(mixed)
    return (unit * phi_cdf(unit)).astype(BF16)


def tap_copies(w_any, w_out, sems, start):
    count = sems.shape[1]
    size = w_out.shape[1] // count
    copies = []
    for g in range(w_out.shape[0]):
        for c in range(count):
            part = pl.ds(c * size, size)
            copies.append(
                pltpu.make_async_copy(
                    w_any.at[start + g, part], w_out.at[g, part], sems.at[g, c]
                )
            )
    for copy in copies:
        copy.start()
    return copies


def five_body(where, *refs, layout, count):
    blocks, stacks = refs[:count], refs[count : count + len(layout)]
    w_any, out, w_out, full, sems, mine, mine_sem = refs[count + len(layout) :]
    own = pltpu.make_async_copy(blocks[0], mine, mine_sem)
    own.start()
    copies = tap_copies(w_any, w_out, sems, 0)
    place_shards(where[0], layout, stacks, 0, 2, full)
    own.wait()
    out[...] = strided([mine[...]] + [b[...] for b in blocks[1:]], full)
    for copy in copies:
        copy.wait()


def six_body(where, act, *refs, layout, count, start):
    stacks = refs[: len(layout)]
    if start is None:
        normed, unit_own, inv_own, full = refs[len(layout) :]
        copies = []
    else:
        w_any, normed, unit_own, inv_own, w_out, full, sems = refs[len(layout) :]
        copies = tap_copies(w_any, w_out, sems, start)
    place_shards(where[0], layout, stacks, 0, 2, full)
    rows = act.shape[0] // count
    act_six = strided([act[e * rows : (e + 1) * rows] for e in range(count)], full)
    unit, inv_dev = normalize(act_six.astype(F32))
    own = rows // 2
    for e in range(count):
        at = pl.multiple_of((where[1] ^ e) * own, own)
        normed[pl.ds(at, own), :] = unit[e * own : (e + 1) * own].astype(BF16)
    unit_own[...] = unit[:own]
    inv_own[...] = jnp.broadcast_to(inv_dev[:own], inv_own.shape)
    for copy in copies:
        copy.wait()


def conv_group(weights, first, wrap, rows):
    size, _, taps = weights.shape
    s = lax.broadcasted_iota(jnp.int32, (rows, taps), 0)
    j = lax.broadcasted_iota(jnp.int32, (rows, taps), 1)
    mask = j < rows - 1 - s
    total = None
    for b in range(0, size, SUB):
        parts = []
        for i in range(b, b + SUB):
            u = jnp.where(mask, wrap[i : i + 1, :], first[i : i + 1, :])
            u = pltpu.roll(u, taps - (rows - 1), 1, stride=1, stride_axis=0)
            parts.append(u.astype(BF16))
        tiles = [weights[i] for i in range(b, b + SUB)]
        term = dot_nt(jnp.concatenate(parts, 1), jnp.concatenate(tiles, 1))
        total = term if total is None else total + term
    return total


def conv(weights, turned, first, wrap, acc, copies=()):
    rows, width = acc.shape[1:]
    start = 0
    for held in weights:
        if held is weights[-1]:
            for copy in copies:
                copy.wait()

        def step(g, carry):
            group = held.at[g]
            if turned is not None:
                turned[...] = jnp.swapaxes(held[g], 0, 1)
                group = turned
            here = pl.ds(pl.multiple_of((start + g) * width, 8), width)
            acc[start + g] = conv_group(group, first.at[here], wrap.at[here], rows)
            return carry

        lax.fori_loop(0, held.shape[0], step, 0)
        start += held.shape[0]
    return jnp.concatenate([acc[g] for g in range(acc.shape[0])], 1)


def forward_body(where, normed, got_a, got_b, *refs, layout, held, late):
    stacks, refs = refs[: len(layout)], refs[len(layout) :]
    weights, refs = list(refs[:held]), refs[held:]
    copies = []
    if late:
        w_any, cot, bias, encoded, slope_rev, proj, w_out, full, first, wrap, acc, sems = refs
        copies = tap_copies(w_any, w_out, sems, acc.shape[0] - late)
        weights.append(w_out)
    else:
        cot, bias, encoded, slope_rev, proj, full, first, wrap, acc = refs
    place_shards(where[0], layout, stacks, 0, 1, full)
    proj[...] = full[0, :, : proj.shape[1]]
    odd = where[0] % 2 == 1
    low = jnp.where(odd, got_a[...], got_b[...])
    high = jnp.where(odd, got_b[...], got_a[...])
    rows = got_a.shape[0]
    chunks = normed.shape[0] // rows
    ext = jnp.concatenate([low, normed[...], high], 0)
    hidden = dot_nn(ext, proj[...]).astype(BF16).astype(F32)
    part = lambda c: hidden[c * rows : (c + 1) * rows]
    flip = flip_rows(rows)
    for c in range(chunks):
        first[...] = jnp.concatenate([part(c), part(c + 1)], 0).T
        wrap[...] = jnp.concatenate([part(c + 2), part(c + 1)], 0).T
        pos = conv(weights, None, first, wrap, acc, copies if c == 0 else ())
        pos = pos + bias[...].astype(F32)
        cdf = phi_cdf(pos)
        here = slice(c * rows, (c + 1) * rows)
        cot_rev = dot_nn(flip, cot[here, :])
        hid_rev = dot_nn(flip, part(c + 1).astype(BF16))
        enc_rev = (hid_rev + pos * cdf).astype(BF16)
        encoded[here, :] = dot_nn(flip, enc_rev).astype(BF16)
        slope = cdf + pos * jnp.exp(-0.5 * pos * pos) * 0.3989422804014327
        slope_rev[here, :] = (cot_rev * slope).astype(BF16)


def backward_body(where, slope_rev, got_a, got_b, *refs, scale, order, held):
    weights, refs = refs[:held], refs[held:]
    (cot, normed, proj), refs = refs[:3], refs[3:]
    kept, sent, unit_grad, unit_sent, first, wrap, acc = refs[:7]
    turned, hid_grad, full, rows_f32 = refs[7:]
    odd = where[0] % 2 == 1
    low = jnp.where(odd, got_a[...], got_b[...])
    high = jnp.where(odd, got_b[...], got_a[...])
    rows = got_a.shape[0]
    chunks = slope_rev.shape[0] // rows
    ext = jnp.concatenate([low, slope_rev[...], high], 0).astype(F32)
    part = lambda c: ext[c * rows : (c + 1) * rows]
    for c in range(chunks):
        first[...] = jnp.concatenate([part(c + 2), part(c + 1)], 0).T
        wrap[...] = jnp.concatenate([part(c), part(c + 1)], 0).T
        back = conv(weights, turned, first, wrap, acc)
        here = slice(c * rows, (c + 1) * rows)
        hid_grad[here, :] = (cot[here, :].astype(F32) + back).astype(BF16)
    grad = hid_grad[...]
    full[...] = (
        dot_nn(normed[...].astype(F32).T.astype(BF16), grad) * scale
    ).reshape(full.shape)
    for n, p in enumerate(order):
        kept[n] = full[where[0] ^ p].astype(BF16)
        sent[n] = full[where[0] ^ (p ^ 1)].astype(BF16)
    slots = rows_f32.shape[0]
    rows_f32[...] = dot_nt(grad, proj[...]).reshape(rows_f32.shape)
    unit_grad[...] = rows_f32[where[1]]
    for e in range(1, slots):
        unit_sent[e - 1] = rows_f32[where[1] ^ e].astype(BF16)


def on_chip(values):
    return [pltpu.with_memory_space_constraint(v, pltpu.VMEM) for v in values]


def in_hbm(value):
    return pltpu.with_memory_space_constraint(value, pltpu.HBM)


def vmem_specs(count):
    return [pl.BlockSpec(memory_space=pltpu.VMEM)] * count


SMEM_SPEC = pl.BlockSpec(memory_space=pltpu.SMEM)
HBM_SPEC = pl.BlockSpec(memory_space=pltpu.HBM)
PARAMS = pltpu.CompilerParams(vmem_limit_bytes=16 * 1024 * 1024)
CONV_PARAMS = pltpu.CompilerParams(vmem_limit_bytes=CONV_MB * 1024 * 1024)


def swap(values, axis, mask):
    count = lax.axis_size(axis)
    return lax.ppermute(values, axis, [(i, i ^ mask) for i in range(count)])


def spread_near(shard, count):
    offs = [n * (count // 4) for n in range(4)]
    pieces = [shard]
    for n in (1, 2, 3):
        pieces.append(swap(shard, "tm", offs[n]))
    return jnp.stack(pieces), offs


def spread_far(stack, offs, count):
    stacks, layout = [stack], [offs]
    mask = count // 8
    while mask >= 1:
        got = []
        for part in stacks:
            got.append(swap(part, "tm", mask))
        stacks = stacks + got
        layout = layout + [[o ^ mask for o in offs] for offs in layout]
        mask //= 2
    return stacks, layout


def halo(tail, head, parity):
    count = lax.axis_size("tm")
    to_a = tail if tail is head else jnp.where(parity == 0, tail, head)
    to_b = tail if tail is head else jnp.where(parity == 0, head, tail)
    pairs = [(2 * i + 1, 2 * i + 2) for i in range(count // 2 - 1)]
    got_b = lax.ppermute(to_b, "tm", pairs + [(b, a) for a, b in pairs])
    got_a = swap(to_a, "tm", 1)
    return got_a, got_b


def on_device(features, weight_five, weight_six, projection, pos_weight, pos_bias, cotangent):
    members, slots = lax.axis_size("tm"), lax.axis_size("grp")
    me, slot = lax.axis_index("tm"), lax.axis_index("grp")
    where = jnp.stack([me, slot]).astype(jnp.int32)
    channels = features.shape[1]
    taps, groups, width = pos_weight.shape[0], pos_weight.shape[1], pos_weight.shape[2]
    columns = groups * width
    half = taps // 2
    own = features.shape[0] // 4
    block = own * slots

    w_taps = in_hbm(jnp.transpose(pos_weight, (1, 2, 3, 0)))
    blocks = [features] + [swap(features, "grp", e) for e in range(1, slots)]
    bias = pos_bias.reshape(1, columns)
    proj_half = lax.dynamic_slice_in_dim(projection, slot * columns, columns, 1)
    proj_half = jnp.pad(proj_half, ((0, 0), (0, channels - columns)))
    five, offs = spread_near(jnp.transpose(weight_five, (0, 2, 1)), members)
    six, _ = spread_near(jnp.transpose(weight_six, (0, 2, 1)), members)
    last, _ = spread_near(proj_half[None], members)
    five, layout = spread_far(five, offs, members)
    six, _ = spread_far(six, offs, members)
    last, _ = spread_far(last, offs, members)
    common = dict(layout=layout)
    taps_scratch = [pltpu.VMEM((2, channels, channels), BF16)]

    cut = 1
    tap_sems = lambda count: pltpu.SemaphoreType.DMA((count, 5))
    act_five, w_low = pl.pallas_call(
        functools.partial(five_body, count=slots, **common),
        in_specs=[SMEM_SPEC, HBM_SPEC] + vmem_specs(slots - 1 + len(five)) + [HBM_SPEC],
        out_specs=vmem_specs(2),
        out_shape=[
            pltpu.VMEM((2 * block, channels), BF16),
            pltpu.VMEM((cut, width, width, taps), BF16),
        ],
        scratch_shapes=taps_scratch
        + [tap_sems(cut), pltpu.VMEM(features.shape, BF16), pltpu.SemaphoreType.DMA(())],
        compiler_params=PARAMS,
        name="five",
    )(where, in_hbm(blocks[0]), *on_chip(blocks[1:] + five), w_taps)
    rest = min(1, groups - cut)
    late = groups - cut - rest
    results = pl.pallas_call(
        functools.partial(six_body, count=slots, start=cut if rest else None, **common),
        in_specs=[SMEM_SPEC] + vmem_specs(1 + len(six)) + ([HBM_SPEC] if rest else []),
        out_specs=vmem_specs(4 if rest else 3),
        out_shape=[
            pltpu.VMEM((block, channels), BF16),
            pltpu.VMEM((own, channels), F32),
            pltpu.VMEM((own, 128), F32),
        ]
        + ([pltpu.VMEM((rest, width, width, taps), BF16)] if rest else []),
        scratch_shapes=taps_scratch + ([tap_sems(rest)] if rest else []),
        compiler_params=PARAMS,
        name="six",
    )(where, act_five, *on_chip(six), *([w_taps] if rest else []))
    normed, unit, inv_dev = results[:3]
    weights = [w_low] + list(results[3:])

    whole = block == half
    tail = normed if whole else normed[block - half :]
    head = normed if whole else normed[:half]
    got_a, got_b = halo(tail, head, me % 2)
    conv_scratch = [
        pltpu.VMEM((columns, taps), F32),
        pltpu.VMEM((columns, taps), F32),
        pltpu.VMEM((groups, half, width), F32),
    ]
    results = pl.pallas_call(
        functools.partial(forward_body, held=len(weights), late=late, **common),
        in_specs=[SMEM_SPEC]
        + vmem_specs(3 + len(last) + len(weights))
        + ([HBM_SPEC] if late else [])
        + vmem_specs(2),
        out_specs=vmem_specs(4 if late else 3),
        out_shape=[
            jax.ShapeDtypeStruct((block, columns), BF16),
            pltpu.VMEM((block, columns), BF16),
            pltpu.VMEM((channels, columns), BF16),
        ]
        + ([pltpu.VMEM((late, width, width, taps), BF16)] if late else []),
        scratch_shapes=[pltpu.VMEM((1, channels, channels), BF16)]
        + conv_scratch
        + ([tap_sems(late)] if late else []),
        compiler_params=CONV_PARAMS,
        name="forward",
    )(
        where, normed, *on_chip([got_a, got_b] + last), *weights,
        *([w_taps] if late else []), cotangent, bias,
    )
    encoded, slope_rev, proj = results[:3]
    weights = weights + list(results[3:])

    tail = slope_rev if whole else slope_rev[block - half :]
    head = slope_rev if whole else slope_rev[:half]
    got_a, got_b = halo(tail, head, me % 2)
    scale = 1.0 / math.sqrt(own * members * slots)
    share = channels // members
    finals = [0, members // 4, members // 2, 3 * (members // 4)]
    masks, mask = [], 2
    while mask < members // 4:
        masks.append(mask)
        mask *= 2
    order = finals
    for mask in reversed(masks):
        order = order + [p ^ mask for p in order]
    kept, sent, unit_grad, unit_sent = pl.pallas_call(
        functools.partial(backward_body, scale=scale, order=order, held=len(weights)),
        in_specs=[SMEM_SPEC] + vmem_specs(6 + len(weights)),
        out_specs=vmem_specs(4),
        out_shape=[pltpu.VMEM((members // 2, share, columns), BF16)] * 2
        + [
            pltpu.VMEM((own, channels), F32),
            pltpu.VMEM((slots - 1, own, channels), BF16),
        ],
        scratch_shapes=conv_scratch
        + [
            pltpu.VMEM((width, width, taps), BF16),
            pltpu.VMEM((block, columns), BF16),
            pltpu.VMEM((members, share, columns), F32),
            pltpu.VMEM((slots, own, channels), F32),
        ],
        compiler_params=CONV_PARAMS,
        name="backward",
    )(where, slope_rev, *on_chip([got_a, got_b]), *weights, cotangent, normed, proj)

    got = swap(sent, "tm", 1)
    total = (kept.astype(F32) + got.astype(F32)).astype(BF16)
    for mask in masks:
        middle = total.shape[0] // 2
        got = swap(total[middle:], "tm", mask)
        total = (total[:middle].astype(F32) + got.astype(F32)).astype(BF16)
    parts = []
    for n in (1, 2, 3):
        parts.append(swap(total[n], "tm", finals[n]))
    projection_grad = total[0].astype(F32) + sum(p.astype(F32) for p in parts)

    grad_unit = unit_grad
    for e in range(1, slots):
        got = swap(unit_sent[e - 1], "grp", e)
        grad_unit = grad_unit + got.astype(F32)
    first_mean = jnp.mean(grad_unit, axis=-1, keepdims=True)
    second_mean = jnp.mean(grad_unit * unit, axis=-1, keepdims=True)
    feature_grad = (inv_dev[:, :1] * (grad_unit - first_mean - unit * second_mean)).astype(BF16)
    return (encoded, feature_grad, projection_grad)


def solution(mesh):
    in_specs = (
        P(("tm", "grp"), None),
        P(None, None, "tm"),
        P(None, None, "tm"),
        P("tm", None),
        P(None, "grp", None, None),
        P("grp"),
        P("tm", "grp"),
    )
    out_specs = (P("tm", "grp"), P(("tm", "grp"), None), P("tm", "grp"))

    return jax.shard_map(
        on_device, mesh=mesh, in_specs=in_specs, out_specs=out_specs, check_vma=False
    )
```

```python
import functools
import math

import jax
import jax.numpy as jnp
from jax import lax
from jax.experimental import pallas as pl
from jax.experimental.pallas import tpu as pltpu
from jax.sharding import PartitionSpec as P


EPS = 1e-05
F32 = jnp.float32
BF16 = jnp.bfloat16
SUB = 8
CONV_MB = 16


def dot_nn(a, b):
    return lax.dot_general(a, b, (((1,), (0,)), ((), ())), preferred_element_type=F32)


def dot_nt(a, b):
    return lax.dot_general(a, b, (((1,), (1,)), ((), ())), preferred_element_type=F32)


def normalize(v):
    average = jnp.mean(v, axis=-1, keepdims=True)
    centred = v - average
    inv_dev = lax.rsqrt(jnp.mean(centred * centred, axis=-1, keepdims=True) + EPS)
    return centred * inv_dev, inv_dev


def phi_cdf(v):
    return 0.5 * (1.0 + lax.erf(v * 0.7071067811865476))


def pick_rows(rows, first):
    r = lax.broadcasted_iota(jnp.int32, (rows, 2 * rows), 0)
    c = lax.broadcasted_iota(jnp.int32, (rows, 2 * rows), 1)
    return jnp.where(c == 2 * r + first, 1.0, 0.0).astype(BF16)


def flip_rows(rows):
    r = lax.broadcasted_iota(jnp.int32, (rows, rows), 0)
    c = lax.broadcasted_iota(jnp.int32, (rows, rows), 1)
    return jnp.where(c == rows - 1 - r, 1.0, 0.0).astype(BF16)


def place_shards(idx, layout, stacks, first, taps, full):
    for offs, ref in zip(layout, stacks):
        width = ref.shape[2]
        for q, off in enumerate(offs):
            at = pl.multiple_of((idx ^ off) * width, width)
            for tap in range(taps):
                full[tap, pl.ds(at, width), :] = ref[q, first + tap]


def strided(blocks, full):
    rows = blocks[0].shape[0] // 2
    even = [dot_nn(pick_rows(rows, 0), b).astype(BF16) for b in blocks]
    odd = [dot_nn(pick_rows(rows, 1), b).astype(BF16) for b in blocks]
    even, odd = jnp.concatenate(even, 0), jnp.concatenate(odd, 0)
    mixed = dot_nt(even, full[0]) + dot_nt(odd, full[1])
    unit, _ = normalize(mixed)
    return (unit * phi_cdf(unit)).astype(BF16)


def hold_body(w_any, w_out, sems):
    count = sems.shape[1]
    size = w_out.shape[1] // count
    copies = []
    for g in range(w_out.shape[0]):
        for c in range(count):
            part = pl.ds(c * size, size)
            copies.append(
                pltpu.make_async_copy(w_any.at[g, part], w_out.at[g, part], sems.at[g, c])
            )
    for copy in copies:
        copy.start()
    for copy in copies:
        copy.wait()


def five_body(where, *refs, layout, count):
    blocks, stacks = refs[:count], refs[count : count + len(layout)]
    out, full, mine, mine_sem = refs[count + len(layout) :]
    own = pltpu.make_async_copy(blocks[0], mine, mine_sem)
    own.start()
    place_shards(where[0], layout, stacks, 0, 2, full)
    own.wait()
    out[...] = strided([mine[...]] + [b[...] for b in blocks[1:]], full)


def six_body(where, act, *refs, layout, count):
    stacks = refs[: len(layout)]
    normed, unit_own, inv_own, full = refs[len(layout) :]
    place_shards(where[0], layout, stacks, 0, 2, full)
    rows = act.shape[0] // count
    act_six = strided([act[e * rows : (e + 1) * rows] for e in range(count)], full)
    unit, inv_dev = normalize(act_six.astype(F32))
    own = rows // 2
    for e in range(count):
        at = pl.multiple_of((where[1] ^ e) * own, own)
        normed[pl.ds(at, own), :] = unit[e * own : (e + 1) * own].astype(BF16)
    unit_own[...] = unit[:own]
    inv_own[...] = jnp.broadcast_to(inv_dev[:own], inv_own.shape)


def conv_group(weights, first, wrap, rows):
    size, _, taps = weights.shape
    s = lax.broadcasted_iota(jnp.int32, (rows, taps), 0)
    j = lax.broadcasted_iota(jnp.int32, (rows, taps), 1)
    mask = j < rows - 1 - s
    total = None
    for b in range(0, size, SUB):
        parts = []
        for i in range(b, b + SUB):
            u = jnp.where(mask, wrap[i : i + 1, :], first[i : i + 1, :])
            u = pltpu.roll(u, taps - (rows - 1), 1, stride=1, stride_axis=0)
            parts.append(u.astype(BF16))
        tiles = [weights[i] for i in range(b, b + SUB)]
        term = dot_nt(jnp.concatenate(parts, 1), jnp.concatenate(tiles, 1))
        total = term if total is None else total + term
    return total


def conv(weights, turned, first, wrap, acc):
    rows, width = acc.shape[1:]

    def step(g, carry):
        group = weights.at[g]
        if turned is not None:
            turned[...] = jnp.swapaxes(weights[g], 0, 1)
            group = turned
        here = pl.ds(pl.multiple_of(g * width, 8), width)
        acc[g] = conv_group(group, first.at[here], wrap.at[here], rows)
        return carry

    lax.fori_loop(0, acc.shape[0], step, 0)
    return jnp.concatenate([acc[g] for g in range(acc.shape[0])], 1)


def forward_body(where, normed, got_a, got_b, *refs, layout):
    stacks, refs = refs[: len(layout)], refs[len(layout) :]
    weights, refs = refs[0], refs[1:]
    cot, bias, encoded, slope_rev, proj, full = refs[:6]
    first, wrap, acc = refs[6:]
    place_shards(where[0], layout, stacks, 2, 1, full)
    proj[...] = full[0, :, : proj.shape[1]]
    odd = where[0] % 2 == 1
    low = jnp.where(odd, got_a[...], got_b[...])
    high = jnp.where(odd, got_b[...], got_a[...])
    rows = got_a.shape[0]
    chunks = normed.shape[0] // rows
    ext = jnp.concatenate([low, normed[...], high], 0)
    hidden = dot_nn(ext, proj[...]).astype(BF16).astype(F32)
    part = lambda c: hidden[c * rows : (c + 1) * rows]
    flip = flip_rows(rows)
    for c in range(chunks):
        first[...] = jnp.concatenate([part(c), part(c + 1)], 0).T
        wrap[...] = jnp.concatenate([part(c + 2), part(c + 1)], 0).T
        pos = conv(weights, None, first, wrap, acc)
        pos = pos + bias[...].astype(F32)
        cdf = phi_cdf(pos)
        here = slice(c * rows, (c + 1) * rows)
        cot_rev = dot_nn(flip, cot[here, :])
        hid_rev = dot_nn(flip, part(c + 1).astype(BF16))
        enc_rev = (hid_rev + pos * cdf).astype(BF16)
        encoded[here, :] = dot_nn(flip, enc_rev).astype(BF16)
        slope = cdf + pos * jnp.exp(-0.5 * pos * pos) * 0.3989422804014327
        slope_rev[here, :] = (cot_rev * slope).astype(BF16)


def backward_body(where, slope_rev, got_a, got_b, *refs, scale, order):
    weights, refs = refs[0], refs[1:]
    (cot, normed, proj), refs = refs[:3], refs[3:]
    kept, sent, unit_grad, unit_sent, first, wrap, acc = refs[:7]
    turned, hid_grad, full, rows_f32 = refs[7:]
    odd = where[0] % 2 == 1
    low = jnp.where(odd, got_a[...], got_b[...])
    high = jnp.where(odd, got_b[...], got_a[...])
    rows = got_a.shape[0]
    chunks = slope_rev.shape[0] // rows
    ext = jnp.concatenate([low, slope_rev[...], high], 0).astype(F32)
    part = lambda c: ext[c * rows : (c + 1) * rows]
    for c in range(chunks):
        first[...] = jnp.concatenate([part(c + 2), part(c + 1)], 0).T
        wrap[...] = jnp.concatenate([part(c), part(c + 1)], 0).T
        back = conv(weights, turned, first, wrap, acc)
        here = slice(c * rows, (c + 1) * rows)
        hid_grad[here, :] = (cot[here, :].astype(F32) + back).astype(BF16)
    grad = hid_grad[...]
    full[...] = (
        dot_nn(normed[...].astype(F32).T.astype(BF16), grad) * scale
    ).reshape(full.shape)
    for n, p in enumerate(order):
        kept[n] = full[where[0] ^ p].astype(BF16)
        sent[n] = full[where[0] ^ (p ^ 1)].astype(BF16)
    slots = rows_f32.shape[0]
    rows_f32[...] = dot_nt(grad, proj[...]).reshape(rows_f32.shape)
    unit_grad[...] = rows_f32[where[1]]
    for e in range(1, slots):
        unit_sent[e - 1] = rows_f32[where[1] ^ e].astype(BF16)


def on_chip(values):
    return [pltpu.with_memory_space_constraint(v, pltpu.VMEM) for v in values]


def in_hbm(value):
    return pltpu.with_memory_space_constraint(value, pltpu.HBM)


def vmem_specs(count):
    return [pl.BlockSpec(memory_space=pltpu.VMEM)] * count


SMEM_SPEC = pl.BlockSpec(memory_space=pltpu.SMEM)
HBM_SPEC = pl.BlockSpec(memory_space=pltpu.HBM)
PARAMS = pltpu.CompilerParams(vmem_limit_bytes=16 * 1024 * 1024)
CONV_PARAMS = pltpu.CompilerParams(vmem_limit_bytes=CONV_MB * 1024 * 1024)


def swap(values, axis, mask):
    count = lax.axis_size(axis)
    return lax.ppermute(values, axis, [(i, i ^ mask) for i in range(count)])


def spread_near(shard, count):
    offs = [n * (count // 4) for n in range(4)]
    pieces = [shard]
    for n in (1, 2, 3):
        pieces.append(swap(shard, "tm", offs[n]))
    return jnp.stack(pieces), offs


def spread_far(stack, offs, count):
    stacks, layout = [stack], [offs]
    mask = count // 8
    while mask >= 1:
        got = []
        for part in stacks:
            got.append(swap(part, "tm", mask))
        stacks = stacks + got
        layout = layout + [[o ^ mask for o in offs] for offs in layout]
        mask //= 2
    return stacks, layout


def halo(tail, head, parity):
    count = lax.axis_size("tm")
    to_a = tail if tail is head else jnp.where(parity == 0, tail, head)
    to_b = tail if tail is head else jnp.where(parity == 0, head, tail)
    pairs = [(2 * i + 1, 2 * i + 2) for i in range(count // 2 - 1)]
    got_b = lax.ppermute(to_b, "tm", pairs + [(b, a) for a, b in pairs])
    got_a = swap(to_a, "tm", 1)
    return got_a, got_b


def on_device(features, weight_five, weight_six, projection, pos_weight, pos_bias, cotangent):
    members, slots = lax.axis_size("tm"), lax.axis_size("grp")
    me, slot = lax.axis_index("tm"), lax.axis_index("grp")
    where = jnp.stack([me, slot]).astype(jnp.int32)
    channels = features.shape[1]
    taps, groups, width = pos_weight.shape[0], pos_weight.shape[1], pos_weight.shape[2]
    columns = groups * width
    half = taps // 2
    own = features.shape[0] // 4
    block = own * slots

    w_taps = in_hbm(jnp.transpose(pos_weight, (1, 2, 3, 0)))
    blocks = [features] + [swap(features, "grp", e) for e in range(1, slots)]
    bias = pos_bias.reshape(1, columns)
    proj_half = lax.dynamic_slice_in_dim(projection, slot * columns, columns, 1)
    proj_half = jnp.pad(proj_half, ((0, 0), (0, channels - columns)))
    rest = jnp.concatenate([jnp.transpose(weight_six, (0, 2, 1)), proj_half[None]], 0)
    five, offs = spread_near(jnp.transpose(weight_five, (0, 2, 1)), members)
    rest, _ = spread_near(rest, members)
    five, layout = spread_far(five, offs, members)
    rest, _ = spread_far(rest, offs, members)
    rest = on_chip(rest)
    common = dict(layout=layout)
    taps_scratch = [pltpu.VMEM((2, channels, channels), BF16)]

    weights = pl.pallas_call(
        hold_body,
        in_specs=[HBM_SPEC],
        out_specs=vmem_specs(1)[0],
        out_shape=pltpu.VMEM((groups, width, width, taps), BF16),
        scratch_shapes=[pltpu.SemaphoreType.DMA((groups, 5))],
        compiler_params=PARAMS,
        name="hold",
    )(w_taps)
    act_five = pl.pallas_call(
        functools.partial(five_body, count=slots, **common),
        in_specs=[SMEM_SPEC, HBM_SPEC] + vmem_specs(slots - 1 + len(five)),
        out_specs=vmem_specs(1)[0],
        out_shape=pltpu.VMEM((2 * block, channels), BF16),
        scratch_shapes=taps_scratch
        + [pltpu.VMEM(features.shape, BF16), pltpu.SemaphoreType.DMA(())],
        compiler_params=PARAMS,
        name="five",
    )(where, in_hbm(blocks[0]), *on_chip(blocks[1:] + five))
    normed, unit, inv_dev = pl.pallas_call(
        functools.partial(six_body, count=slots, **common),
        in_specs=[SMEM_SPEC] + vmem_specs(1 + len(rest)),
        out_specs=vmem_specs(3),
        out_shape=[
            pltpu.VMEM((block, channels), BF16),
            pltpu.VMEM((own, channels), F32),
            pltpu.VMEM((own, 128), F32),
        ],
        scratch_shapes=taps_scratch,
        compiler_params=PARAMS,
        name="six",
    )(where, act_five, *rest)

    whole = block == half
    tail = normed if whole else normed[block - half :]
    head = normed if whole else normed[:half]
    got_a, got_b = halo(tail, head, me % 2)
    conv_scratch = [
        pltpu.VMEM((columns, taps), F32),
        pltpu.VMEM((columns, taps), F32),
        pltpu.VMEM((groups, half, width), F32),
    ]
    encoded, slope_rev, proj = pl.pallas_call(
        functools.partial(forward_body, **common),
        in_specs=[SMEM_SPEC] + vmem_specs(3 + len(rest) + 3),
        out_specs=vmem_specs(3),
        out_shape=[
            jax.ShapeDtypeStruct((block, columns), BF16),
            pltpu.VMEM((block, columns), BF16),
            pltpu.VMEM((channels, columns), BF16),
        ],
        scratch_shapes=[pltpu.VMEM((1, channels, channels), BF16)] + conv_scratch,
        compiler_params=CONV_PARAMS,
        name="forward",
    )(where, normed, *on_chip([got_a, got_b]), *rest, weights, cotangent, bias)

    tail = slope_rev if whole else slope_rev[block - half :]
    head = slope_rev if whole else slope_rev[:half]
    got_a, got_b = halo(tail, head, me % 2)
    scale = 1.0 / math.sqrt(own * members * slots)
    share = channels // members
    finals = [0, members // 4, members // 2, 3 * (members // 4)]
    masks, mask = [], 2
    while mask < members // 4:
        masks.append(mask)
        mask *= 2
    order = finals
    for mask in reversed(masks):
        order = order + [p ^ mask for p in order]
    kept, sent, unit_grad, unit_sent = pl.pallas_call(
        functools.partial(backward_body, scale=scale, order=order),
        in_specs=[SMEM_SPEC] + vmem_specs(7),
        out_specs=vmem_specs(4),
        out_shape=[pltpu.VMEM((members // 2, share, columns), BF16)] * 2
        + [
            pltpu.VMEM((own, channels), F32),
            pltpu.VMEM((slots - 1, own, channels), BF16),
        ],
        scratch_shapes=conv_scratch
        + [
            pltpu.VMEM((width, width, taps), BF16),
            pltpu.VMEM((block, columns), BF16),
            pltpu.VMEM((members, share, columns), F32),
            pltpu.VMEM((slots, own, channels), F32),
        ],
        compiler_params=CONV_PARAMS,
        name="backward",
    )(where, slope_rev, *on_chip([got_a, got_b]), weights, cotangent, normed, proj)

    got = swap(sent, "tm", 1)
    total = (kept.astype(F32) + got.astype(F32)).astype(BF16)
    for mask in masks:
        middle = total.shape[0] // 2
        got = swap(total[middle:], "tm", mask)
        total = (total[:middle].astype(F32) + got.astype(F32)).astype(BF16)
    parts = []
    for n in (1, 2, 3):
        parts.append(swap(total[n], "tm", finals[n]))
    projection_grad = total[0].astype(F32) + sum(p.astype(F32) for p in parts)

    grad_unit = unit_grad
    for e in range(1, slots):
        got = swap(unit_sent[e - 1], "grp", e)
        grad_unit = grad_unit + got.astype(F32)
    first_mean = jnp.mean(grad_unit, axis=-1, keepdims=True)
    second_mean = jnp.mean(grad_unit * unit, axis=-1, keepdims=True)
    feature_grad = (inv_dev[:, :1] * (grad_unit - first_mean - unit * second_mean)).astype(BF16)
    return (encoded, feature_grad, projection_grad)


def solution(mesh):
    in_specs = (
        P(("tm", "grp"), None),
        P(None, None, "tm"),
        P(None, None, "tm"),
        P("tm", None),
        P(None, "grp", None, None),
        P("grp"),
        P("tm", "grp"),
    )
    out_specs = (P("tm", "grp"), P(("tm", "grp"), None), P("tm", "grp"))

    return jax.shard_map(
        on_device, mesh=mesh, in_specs=in_specs, out_specs=out_specs, check_vma=False
    )
```

```python
import functools
import math

import jax
import jax.numpy as jnp
from jax import lax
from jax.experimental import pallas as pl
from jax.experimental.pallas import tpu as pltpu
from jax.sharding import PartitionSpec as P


EPS = 1e-05
F32 = jnp.float32
BF16 = jnp.bfloat16
SUB = 8
CONV_MB = 16


def dot_nn(a, b):
    return lax.dot_general(a, b, (((1,), (0,)), ((), ())), preferred_element_type=F32)


def dot_nt(a, b):
    return lax.dot_general(a, b, (((1,), (1,)), ((), ())), preferred_element_type=F32)


def normalize(v):
    average = jnp.mean(v, axis=-1, keepdims=True)
    centred = v - average
    inv_dev = lax.rsqrt(jnp.mean(centred * centred, axis=-1, keepdims=True) + EPS)
    return centred * inv_dev, inv_dev


def phi_cdf(v):
    return 0.5 * (1.0 + lax.erf(v * 0.7071067811865476))


def pick_rows(rows, first):
    r = lax.broadcasted_iota(jnp.int32, (rows, 2 * rows), 0)
    c = lax.broadcasted_iota(jnp.int32, (rows, 2 * rows), 1)
    return jnp.where(c == 2 * r + first, 1.0, 0.0).astype(BF16)


def flip_rows(rows):
    r = lax.broadcasted_iota(jnp.int32, (rows, rows), 0)
    c = lax.broadcasted_iota(jnp.int32, (rows, rows), 1)
    return jnp.where(c == rows - 1 - r, 1.0, 0.0).astype(BF16)


def place_shards(idx, layout, stacks, first, taps, full):
    for offs, ref in zip(layout, stacks):
        width = ref.shape[2]
        for q, off in enumerate(offs):
            at = pl.multiple_of((idx ^ off) * width, width)
            for tap in range(taps):
                full[tap, pl.ds(at, width), :] = ref[q, first + tap]


def strided(blocks, full):
    rows = blocks[0].shape[0] // 2
    even = [dot_nn(pick_rows(rows, 0), b).astype(BF16) for b in blocks]
    odd = [dot_nn(pick_rows(rows, 1), b).astype(BF16) for b in blocks]
    even, odd = jnp.concatenate(even, 0), jnp.concatenate(odd, 0)
    mixed = dot_nt(even, full[0]) + dot_nt(odd, full[1])
    unit, _ = normalize(mixed)
    return (unit * phi_cdf(unit)).astype(BF16)


def tap_copies(w_any, w_out, sems, start):
    count = sems.shape[1]
    size = w_out.shape[1] // count
    copies = []
    for g in range(w_out.shape[0]):
        for c in range(count):
            part = pl.ds(c * size, size)
            copies.append(
                pltpu.make_async_copy(
                    w_any.at[start + g, part], w_out.at[g, part], sems.at[g, c]
                )
            )
    for copy in copies:
        copy.start()
    return copies


def five_body(where, *refs, layout, count):
    blocks, stacks = refs[:count], refs[count : count + len(layout)]
    w_any, out, w_out, full, sems, mine, mine_sem = refs[count + len(layout) :]
    own = pltpu.make_async_copy(blocks[0], mine, mine_sem)
    own.start()
    copies = tap_copies(w_any, w_out, sems, 0)
    place_shards(where[0], layout, stacks, 0, 2, full)
    own.wait()
    out[...] = strided([mine[...]] + [b[...] for b in blocks[1:]], full)
    for copy in copies:
        copy.wait()


def six_body(where, act, *refs, layout, count, start):
    stacks = refs[: len(layout)]
    if start is None:
        normed, unit_own, inv_own, full = refs[len(layout) :]
        copies = []
    else:
        w_any, normed, unit_own, inv_own, w_out, full, sems = refs[len(layout) :]
        copies = tap_copies(w_any, w_out, sems, start)
    place_shards(where[0], layout, stacks, 0, 2, full)
    rows = act.shape[0] // count
    act_six = strided([act[e * rows : (e + 1) * rows] for e in range(count)], full)
    unit, inv_dev = normalize(act_six.astype(F32))
    own = rows // 2
    for e in range(count):
        at = pl.multiple_of((where[1] ^ e) * own, own)
        normed[pl.ds(at, own), :] = unit[e * own : (e + 1) * own].astype(BF16)
    unit_own[...] = unit[:own]
    inv_own[...] = jnp.broadcast_to(inv_dev[:own], inv_own.shape)
    for copy in copies:
        copy.wait()


def conv_group(weights, first, wrap, rows):
    size, _, taps = weights.shape
    s = lax.broadcasted_iota(jnp.int32, (rows, taps), 0)
    j = lax.broadcasted_iota(jnp.int32, (rows, taps), 1)
    mask = j < rows - 1 - s
    total = None
    for b in range(0, size, SUB):
        parts = []
        for i in range(b, b + SUB):
            u = jnp.where(mask, wrap[i : i + 1, :], first[i : i + 1, :])
            u = pltpu.roll(u, taps - (rows - 1), 1, stride=1, stride_axis=0)
            parts.append(u.astype(BF16))
        tiles = [weights[i] for i in range(b, b + SUB)]
        term = dot_nt(jnp.concatenate(parts, 1), jnp.concatenate(tiles, 1))
        total = term if total is None else total + term
    return total


def conv(weights, turned, first, wrap, acc):
    rows, width = acc.shape[1:]
    start = 0
    for held in weights:
        def step(g, carry):
            group = held.at[g]
            if turned is not None:
                turned[...] = jnp.swapaxes(held[g], 0, 1)
                group = turned
            here = pl.ds(pl.multiple_of((start + g) * width, 8), width)
            acc[start + g] = conv_group(group, first.at[here], wrap.at[here], rows)
            return carry

        lax.fori_loop(0, held.shape[0], step, 0)
        start += held.shape[0]
    return jnp.concatenate([acc[g] for g in range(acc.shape[0])], 1)


def forward_body(where, normed, got_a, got_b, *refs, layout, held):
    stacks, refs = refs[: len(layout)], refs[len(layout) :]
    weights, refs = refs[:held], refs[held:]
    cot, bias, encoded, slope_rev, proj, full = refs[:6]
    first, wrap, acc = refs[6:]
    place_shards(where[0], layout, stacks, 0, 1, full)
    proj[...] = full[0, :, : proj.shape[1]]
    odd = where[0] % 2 == 1
    low = jnp.where(odd, got_a[...], got_b[...])
    high = jnp.where(odd, got_b[...], got_a[...])
    rows = got_a.shape[0]
    chunks = normed.shape[0] // rows
    ext = jnp.concatenate([low, normed[...], high], 0)
    hidden = dot_nn(ext, proj[...]).astype(BF16).astype(F32)
    part = lambda c: hidden[c * rows : (c + 1) * rows]
    flip = flip_rows(rows)
    for c in range(chunks):
        first[...] = jnp.concatenate([part(c), part(c + 1)], 0).T
        wrap[...] = jnp.concatenate([part(c + 2), part(c + 1)], 0).T
        pos = conv(weights, None, first, wrap, acc)
        pos = pos + bias[...].astype(F32)
        cdf = phi_cdf(pos)
        here = slice(c * rows, (c + 1) * rows)
        cot_rev = dot_nn(flip, cot[here, :])
        hid_rev = dot_nn(flip, part(c + 1).astype(BF16))
        enc_rev = (hid_rev + pos * cdf).astype(BF16)
        encoded[here, :] = dot_nn(flip, enc_rev).astype(BF16)
        slope = cdf + pos * jnp.exp(-0.5 * pos * pos) * 0.3989422804014327
        slope_rev[here, :] = (cot_rev * slope).astype(BF16)


def backward_body(where, slope_rev, got_a, got_b, *refs, scale, order, held):
    weights, refs = refs[:held], refs[held:]
    (cot, normed, proj), refs = refs[:3], refs[3:]
    kept, sent, unit_grad, unit_sent, first, wrap, acc = refs[:7]
    turned, hid_grad, full, rows_f32 = refs[7:]
    odd = where[0] % 2 == 1
    low = jnp.where(odd, got_a[...], got_b[...])
    high = jnp.where(odd, got_b[...], got_a[...])
    rows = got_a.shape[0]
    chunks = slope_rev.shape[0] // rows
    ext = jnp.concatenate([low, slope_rev[...], high], 0).astype(F32)
    part = lambda c: ext[c * rows : (c + 1) * rows]
    for c in range(chunks):
        first[...] = jnp.concatenate([part(c + 2), part(c + 1)], 0).T
        wrap[...] = jnp.concatenate([part(c), part(c + 1)], 0).T
        back = conv(weights, turned, first, wrap, acc)
        here = slice(c * rows, (c + 1) * rows)
        hid_grad[here, :] = (cot[here, :].astype(F32) + back).astype(BF16)
    grad = hid_grad[...]
    full[...] = (
        dot_nn(normed[...].astype(F32).T.astype(BF16), grad) * scale
    ).reshape(full.shape)
    for n, p in enumerate(order):
        kept[n] = full[where[0] ^ p].astype(BF16)
        sent[n] = full[where[0] ^ (p ^ 1)].astype(BF16)
    slots = rows_f32.shape[0]
    rows_f32[...] = dot_nt(grad, proj[...]).reshape(rows_f32.shape)
    unit_grad[...] = rows_f32[where[1]]
    for e in range(1, slots):
        unit_sent[e - 1] = rows_f32[where[1] ^ e].astype(BF16)


def on_chip(values):
    return [pltpu.with_memory_space_constraint(v, pltpu.VMEM) for v in values]


def in_hbm(value):
    return pltpu.with_memory_space_constraint(value, pltpu.HBM)


def vmem_specs(count):
    return [pl.BlockSpec(memory_space=pltpu.VMEM)] * count


SMEM_SPEC = pl.BlockSpec(memory_space=pltpu.SMEM)
HBM_SPEC = pl.BlockSpec(memory_space=pltpu.HBM)
PARAMS = pltpu.CompilerParams(vmem_limit_bytes=16 * 1024 * 1024)
CONV_PARAMS = pltpu.CompilerParams(vmem_limit_bytes=CONV_MB * 1024 * 1024)


def swap(values, axis, mask):
    count = lax.axis_size(axis)
    return lax.ppermute(values, axis, [(i, i ^ mask) for i in range(count)])


def spread_near(shard, count):
    offs = [n * (count // 4) for n in range(4)]
    pieces = [shard]
    for n in (1, 2, 3):
        pieces.append(swap(shard, "tm", offs[n]))
    return jnp.stack(pieces), offs


def spread_doubling(shard, count):
    stack, offs = shard[None], [0]
    for mask in (count // 2, count // 4):
        got = swap(stack, "tm", mask)
        stack = jnp.concatenate([stack, got], 0)
        offs = offs + [o ^ mask for o in offs]
    return stack, offs


def spread_far(stack, offs, count):
    stacks, layout = [stack], [offs]
    mask = count // 8
    while mask >= 1:
        got = []
        for part in stacks:
            got.append(swap(part, "tm", mask))
        stacks = stacks + got
        layout = layout + [[o ^ mask for o in offs] for offs in layout]
        mask //= 2
    return stacks, layout


def halo(tail, head, parity):
    count = lax.axis_size("tm")
    to_a = tail if tail is head else jnp.where(parity == 0, tail, head)
    to_b = tail if tail is head else jnp.where(parity == 0, head, tail)
    pairs = [(2 * i + 1, 2 * i + 2) for i in range(count // 2 - 1)]
    got_b = lax.ppermute(to_b, "tm", pairs + [(b, a) for a, b in pairs])
    got_a = swap(to_a, "tm", 1)
    return got_a, got_b


def on_device(features, weight_five, weight_six, projection, pos_weight, pos_bias, cotangent):
    members, slots = lax.axis_size("tm"), lax.axis_size("grp")
    me, slot = lax.axis_index("tm"), lax.axis_index("grp")
    where = jnp.stack([me, slot]).astype(jnp.int32)
    channels = features.shape[1]
    taps, groups, width = pos_weight.shape[0], pos_weight.shape[1], pos_weight.shape[2]
    columns = groups * width
    half = taps // 2
    own = features.shape[0] // 4
    block = own * slots

    w_taps = in_hbm(jnp.transpose(pos_weight, (1, 2, 3, 0)))
    blocks = [features] + [swap(features, "grp", e) for e in range(1, slots)]
    bias = pos_bias.reshape(1, columns)
    proj_half = lax.dynamic_slice_in_dim(projection, slot * columns, columns, 1)
    proj_half = jnp.pad(proj_half, ((0, 0), (0, channels - columns)))
    five, offs = spread_near(jnp.transpose(weight_five, (0, 2, 1)), members)
    six, _ = spread_near(jnp.transpose(weight_six, (0, 2, 1)), members)
    last, last_offs = spread_doubling(proj_half[None], members)
    five, layout = spread_far(five, offs, members)
    six, _ = spread_far(six, offs, members)
    last, last_layout = spread_far(last, last_offs, members)
    common = dict(layout=layout)
    taps_scratch = [pltpu.VMEM((2, channels, channels), BF16)]

    cut = max(1, groups - 1)
    tap_sems = lambda count: pltpu.SemaphoreType.DMA((count, 5))
    act_five, w_low = pl.pallas_call(
        functools.partial(five_body, count=slots, **common),
        in_specs=[SMEM_SPEC, HBM_SPEC] + vmem_specs(slots - 1 + len(five)) + [HBM_SPEC],
        out_specs=vmem_specs(2),
        out_shape=[
            pltpu.VMEM((2 * block, channels), BF16),
            pltpu.VMEM((cut, width, width, taps), BF16),
        ],
        scratch_shapes=taps_scratch
        + [tap_sems(cut), pltpu.VMEM(features.shape, BF16), pltpu.SemaphoreType.DMA(())],
        compiler_params=PARAMS,
        name="five",
    )(where, in_hbm(blocks[0]), *on_chip(blocks[1:] + five), w_taps)
    rest = groups - cut
    results = pl.pallas_call(
        functools.partial(six_body, count=slots, start=cut if rest else None, **common),
        in_specs=[SMEM_SPEC] + vmem_specs(1 + len(six)) + ([HBM_SPEC] if rest else []),
        out_specs=vmem_specs(4 if rest else 3),
        out_shape=[
            pltpu.VMEM((block, channels), BF16),
            pltpu.VMEM((own, channels), F32),
            pltpu.VMEM((own, 128), F32),
        ]
        + ([pltpu.VMEM((rest, width, width, taps), BF16)] if rest else []),
        scratch_shapes=taps_scratch + ([tap_sems(rest)] if rest else []),
        compiler_params=PARAMS,
        name="six",
    )(where, act_five, *on_chip(six), *([w_taps] if rest else []))
    normed, unit, inv_dev = results[:3]
    weights = [w_low] + list(results[3:])

    whole = block == half
    tail = normed if whole else normed[block - half :]
    head = normed if whole else normed[:half]
    got_a, got_b = halo(tail, head, me % 2)
    conv_scratch = [
        pltpu.VMEM((columns, taps), F32),
        pltpu.VMEM((columns, taps), F32),
        pltpu.VMEM((groups, half, width), F32),
    ]
    encoded, slope_rev, proj = pl.pallas_call(
        functools.partial(forward_body, held=len(weights), layout=last_layout),
        in_specs=[SMEM_SPEC] + vmem_specs(3 + len(last) + len(weights) + 2),
        out_specs=vmem_specs(3),
        out_shape=[
            jax.ShapeDtypeStruct((block, columns), BF16),
            pltpu.VMEM((block, columns), BF16),
            pltpu.VMEM((channels, columns), BF16),
        ],
        scratch_shapes=[pltpu.VMEM((1, channels, channels), BF16)] + conv_scratch,
        compiler_params=CONV_PARAMS,
        name="forward",
    )(where, normed, *on_chip([got_a, got_b] + last), *weights, cotangent, bias)

    tail = slope_rev if whole else slope_rev[block - half :]
    head = slope_rev if whole else slope_rev[:half]
    got_a, got_b = halo(tail, head, me % 2)
    scale = 1.0 / math.sqrt(own * members * slots)
    share = channels // members
    finals = [0, members // 4, members // 2, 3 * (members // 4)]
    masks, mask = [], 2
    while mask < members // 4:
        masks.append(mask)
        mask *= 2
    order = finals
    for mask in reversed(masks):
        order = order + [p ^ mask for p in order]
    kept, sent, unit_grad, unit_sent = pl.pallas_call(
        functools.partial(backward_body, scale=scale, order=order, held=len(weights)),
        in_specs=[SMEM_SPEC] + vmem_specs(6 + len(weights)),
        out_specs=vmem_specs(4),
        out_shape=[pltpu.VMEM((members // 2, share, columns), BF16)] * 2
        + [
            pltpu.VMEM((own, channels), F32),
            pltpu.VMEM((slots - 1, own, channels), BF16),
        ],
        scratch_shapes=conv_scratch
        + [
            pltpu.VMEM((width, width, taps), BF16),
            pltpu.VMEM((block, columns), BF16),
            pltpu.VMEM((members, share, columns), F32),
            pltpu.VMEM((slots, own, channels), F32),
        ],
        compiler_params=CONV_PARAMS,
        name="backward",
    )(where, slope_rev, *on_chip([got_a, got_b]), *weights, cotangent, normed, proj)

    got = swap(sent, "tm", 1)
    total = (kept.astype(F32) + got.astype(F32)).astype(BF16)
    for mask in masks:
        middle = total.shape[0] // 2
        got = swap(total[middle:], "tm", mask)
        total = (total[:middle].astype(F32) + got.astype(F32)).astype(BF16)
    parts = []
    for n in (1, 2, 3):
        parts.append(swap(total[n], "tm", finals[n]))
    projection_grad = total[0].astype(F32) + sum(p.astype(F32) for p in parts)

    grad_unit = unit_grad
    for e in range(1, slots):
        got = swap(unit_sent[e - 1], "grp", e)
        grad_unit = grad_unit + got.astype(F32)
    first_mean = jnp.mean(grad_unit, axis=-1, keepdims=True)
    second_mean = jnp.mean(grad_unit * unit, axis=-1, keepdims=True)
    feature_grad = (inv_dev[:, :1] * (grad_unit - first_mean - unit * second_mean)).astype(BF16)
    return (encoded, feature_grad, projection_grad)


def solution(mesh):
    in_specs = (
        P(("tm", "grp"), None),
        P(None, None, "tm"),
        P(None, None, "tm"),
        P("tm", None),
        P(None, "grp", None, None),
        P("grp"),
        P("tm", "grp"),
    )
    out_specs = (P("tm", "grp"), P(("tm", "grp"), None), P("tm", "grp"))

    return jax.shard_map(
        on_device, mesh=mesh, in_specs=in_specs, out_specs=out_specs, check_vma=False
    )
```

```python
import functools
import math

import jax
import jax.numpy as jnp
from jax import lax
from jax.experimental import pallas as pl
from jax.experimental.pallas import tpu as pltpu
from jax.sharding import PartitionSpec as P


EPS = 1e-05
F32 = jnp.float32
BF16 = jnp.bfloat16
SUB = 8
CONV_MB = 16


def dot_nn(a, b):
    return lax.dot_general(a, b, (((1,), (0,)), ((), ())), preferred_element_type=F32)


def dot_nt(a, b):
    return lax.dot_general(a, b, (((1,), (1,)), ((), ())), preferred_element_type=F32)


def normalize(v):
    average = jnp.mean(v, axis=-1, keepdims=True)
    centred = v - average
    inv_dev = lax.rsqrt(jnp.mean(centred * centred, axis=-1, keepdims=True) + EPS)
    return centred * inv_dev, inv_dev


def phi_cdf(v):
    return 0.5 * (1.0 + lax.erf(v * 0.7071067811865476))


def pick_rows(rows, first):
    r = lax.broadcasted_iota(jnp.int32, (rows, 2 * rows), 0)
    c = lax.broadcasted_iota(jnp.int32, (rows, 2 * rows), 1)
    return jnp.where(c == 2 * r + first, 1.0, 0.0).astype(BF16)


def flip_rows(rows):
    r = lax.broadcasted_iota(jnp.int32, (rows, rows), 0)
    c = lax.broadcasted_iota(jnp.int32, (rows, rows), 1)
    return jnp.where(c == rows - 1 - r, 1.0, 0.0).astype(BF16)


def place_shards(idx, layout, stacks, first, taps, full):
    for offs, ref in zip(layout, stacks):
        width = ref.shape[2]
        for q, off in enumerate(offs):
            at = pl.multiple_of((idx ^ off) * width, width)
            for tap in range(taps):
                full[tap, pl.ds(at, width), :] = ref[q, first + tap]


def strided(blocks, full):
    rows = blocks[0].shape[0] // 2
    even = [dot_nn(pick_rows(rows, 0), b).astype(BF16) for b in blocks]
    odd = [dot_nn(pick_rows(rows, 1), b).astype(BF16) for b in blocks]
    even, odd = jnp.concatenate(even, 0), jnp.concatenate(odd, 0)
    mixed = dot_nt(even, full[0]) + dot_nt(odd, full[1])
    unit, _ = normalize(mixed)
    return (unit * phi_cdf(unit)).astype(BF16)


def tap_copies(w_any, w_out, sems, start):
    count = sems.shape[1]
    size = w_out.shape[1] // count
    copies = []
    for g in range(w_out.shape[0]):
        for c in range(count):
            part = pl.ds(c * size, size)
            copies.append(
                pltpu.make_async_copy(
                    w_any.at[start + g, part], w_out.at[g, part], sems.at[g, c]
                )
            )
    for copy in copies:
        copy.start()
    return copies


def five_body(where, *refs, layout, count):
    blocks, stacks = refs[:count], refs[count : count + len(layout)]
    w_any, out, w_out, full, sems, mine, mine_sem = refs[count + len(layout) :]
    own = pltpu.make_async_copy(blocks[0], mine, mine_sem)
    own.start()
    copies = tap_copies(w_any, w_out, sems, 0)
    place_shards(where[0], layout, stacks, 0, 2, full)
    own.wait()
    out[...] = strided([mine[...]] + [b[...] for b in blocks[1:]], full)
    for copy in copies:
        copy.wait()


def six_body(where, act, *refs, layout, count, start):
    stacks = refs[: len(layout)]
    if start is None:
        normed, unit_own, inv_own, full = refs[len(layout) :]
        copies = []
    else:
        w_any, normed, unit_own, inv_own, w_out, full, sems = refs[len(layout) :]
        copies = tap_copies(w_any, w_out, sems, start)
    place_shards(where[0], layout, stacks, 0, 2, full)
    rows = act.shape[0] // count
    act_six = strided([act[e * rows : (e + 1) * rows] for e in range(count)], full)
    unit, inv_dev = normalize(act_six.astype(F32))
    own = rows // 2
    for e in range(count):
        at = pl.multiple_of((where[1] ^ e) * own, own)
        normed[pl.ds(at, own), :] = unit[e * own : (e + 1) * own].astype(BF16)
    unit_own[...] = unit[:own]
    inv_own[...] = jnp.broadcast_to(inv_dev[:own], inv_own.shape)
    for copy in copies:
        copy.wait()


def conv_group(weights, first, wrap, rows):
    size, _, taps = weights.shape
    s = lax.broadcasted_iota(jnp.int32, (rows, taps), 0)
    j = lax.broadcasted_iota(jnp.int32, (rows, taps), 1)
    mask = j < rows - 1 - s
    total = None
    for b in range(0, size, SUB):
        parts = []
        for i in range(b, b + SUB):
            u = jnp.where(mask, wrap[i : i + 1, :], first[i : i + 1, :])
            u = pltpu.roll(u, taps - (rows - 1), 1, stride=1, stride_axis=0)
            parts.append(u.astype(BF16))
        tiles = [weights[i] for i in range(b, b + SUB)]
        term = dot_nt(jnp.concatenate(parts, 1), jnp.concatenate(tiles, 1))
        total = term if total is None else total + term
    return total


def conv(weights, turned, first, wrap, acc):
    rows, width = acc.shape[1:]
    start = 0
    for held in weights:
        def step(g, carry):
            group = held.at[g]
            if turned is not None:
                turned[...] = jnp.swapaxes(held[g], 0, 1)
                group = turned
            here = pl.ds(pl.multiple_of((start + g) * width, 8), width)
            acc[start + g] = conv_group(group, first.at[here], wrap.at[here], rows)
            return carry

        lax.fori_loop(0, held.shape[0], step, 0)
        start += held.shape[0]
    return jnp.concatenate([acc[g] for g in range(acc.shape[0])], 1)


def forward_body(where, normed, got_a, got_b, *refs, layout, held):
    stacks, refs = refs[: len(layout)], refs[len(layout) :]
    weights, refs = refs[:held], refs[held:]
    cot, bias, encoded, slope_rev, proj, full = refs[:6]
    first, wrap, acc = refs[6:]
    place_shards(where[0], layout, stacks, 0, 1, full)
    proj[...] = full[0, :, : proj.shape[1]]
    odd = where[0] % 2 == 1
    low = jnp.where(odd, got_a[...], got_b[...])
    high = jnp.where(odd, got_b[...], got_a[...])
    rows = got_a.shape[0]
    chunks = normed.shape[0] // rows
    ext = jnp.concatenate([low, normed[...], high], 0)
    hidden = dot_nn(ext, proj[...]).astype(BF16).astype(F32)
    part = lambda c: hidden[c * rows : (c + 1) * rows]
    flip = flip_rows(rows)
    for c in range(chunks):
        first[...] = jnp.concatenate([part(c), part(c + 1)], 0).T
        wrap[...] = jnp.concatenate([part(c + 2), part(c + 1)], 0).T
        pos = conv(weights, None, first, wrap, acc)
        pos = pos + bias[...].astype(F32)
        cdf = phi_cdf(pos)
        here = slice(c * rows, (c + 1) * rows)
        cot_rev = dot_nn(flip, cot[here, :])
        hid_rev = dot_nn(flip, part(c + 1).astype(BF16))
        enc_rev = (hid_rev + pos * cdf).astype(BF16)
        encoded[here, :] = dot_nn(flip, enc_rev).astype(BF16)
        slope = cdf + pos * jnp.exp(-0.5 * pos * pos) * 0.3989422804014327
        slope_rev[here, :] = (cot_rev * slope).astype(BF16)


def backward_body(where, slope_rev, got_a, got_b, *refs, scale, order, held):
    weights, refs = refs[:held], refs[held:]
    (cot, normed, proj), refs = refs[:3], refs[3:]
    kept, sent, unit_grad, unit_sent, first, wrap, acc = refs[:7]
    turned, hid_grad, full, rows_f32 = refs[7:]
    odd = where[0] % 2 == 1
    low = jnp.where(odd, got_a[...], got_b[...])
    high = jnp.where(odd, got_b[...], got_a[...])
    rows = got_a.shape[0]
    chunks = slope_rev.shape[0] // rows
    ext = jnp.concatenate([low, slope_rev[...], high], 0).astype(F32)
    part = lambda c: ext[c * rows : (c + 1) * rows]
    for c in range(chunks):
        first[...] = jnp.concatenate([part(c + 2), part(c + 1)], 0).T
        wrap[...] = jnp.concatenate([part(c), part(c + 1)], 0).T
        back = conv(weights, turned, first, wrap, acc)
        here = slice(c * rows, (c + 1) * rows)
        hid_grad[here, :] = (cot[here, :].astype(F32) + back).astype(BF16)
    grad = hid_grad[...]
    full[...] = (
        dot_nn(normed[...].astype(F32).T.astype(BF16), grad) * scale
    ).reshape(full.shape)
    for n, p in enumerate(order):
        kept[n] = full[where[0] ^ p].astype(BF16)
        sent[n] = full[where[0] ^ (p ^ 1)].astype(BF16)
    slots = rows_f32.shape[0]
    rows_f32[...] = dot_nt(grad, proj[...]).reshape(rows_f32.shape)
    unit_grad[...] = rows_f32[where[1]]
    for e in range(1, slots):
        unit_sent[e - 1] = rows_f32[where[1] ^ e].astype(BF16)


def on_chip(values):
    return [pltpu.with_memory_space_constraint(v, pltpu.VMEM) for v in values]


def in_hbm(value):
    return pltpu.with_memory_space_constraint(value, pltpu.HBM)


def vmem_specs(count):
    return [pl.BlockSpec(memory_space=pltpu.VMEM)] * count


SMEM_SPEC = pl.BlockSpec(memory_space=pltpu.SMEM)
HBM_SPEC = pl.BlockSpec(memory_space=pltpu.HBM)
PARAMS = pltpu.CompilerParams(vmem_limit_bytes=16 * 1024 * 1024)
CONV_PARAMS = pltpu.CompilerParams(vmem_limit_bytes=CONV_MB * 1024 * 1024)


def swap(values, axis, mask):
    count = lax.axis_size(axis)
    return lax.ppermute(values, axis, [(i, i ^ mask) for i in range(count)])


def spread_near(shard, count):
    offs = [n * (count // 4) for n in range(4)]
    pieces = [shard]
    for n in (1, 2, 3):
        pieces.append(swap(shard, "tm", offs[n]))
    stack = jnp.stack(pieces)
    return stack, offs


def spread_doubling(shard, count):
    stack, offs = shard[None], [0]
    for mask in (count // 2, count // 4):
        got = swap(stack, "tm", mask)
        stack = jnp.concatenate([stack, got], 0)
        offs = offs + [o ^ mask for o in offs]
    return stack, offs


def spread_far(stack, offs, count):
    stacks, layout = [stack], [offs]
    mask = count // 8
    while mask >= 1:
        got = []
        for part in stacks:
            got.append(swap(part, "tm", mask))
        stacks = stacks + got
        layout = layout + [[o ^ mask for o in offs] for offs in layout]
        mask //= 2
    return stacks, layout


def halo(tail, head, parity):
    count = lax.axis_size("tm")
    to_a = tail if tail is head else jnp.where(parity == 0, tail, head)
    to_b = tail if tail is head else jnp.where(parity == 0, head, tail)
    pairs = [(2 * i + 1, 2 * i + 2) for i in range(count // 2 - 1)]
    got_b = lax.ppermute(to_b, "tm", pairs + [(b, a) for a, b in pairs])
    got_a = swap(to_a, "tm", 1)
    return got_a, got_b


def on_device(features, weight_five, weight_six, projection, pos_weight, pos_bias, cotangent):
    members, slots = lax.axis_size("tm"), lax.axis_size("grp")
    me, slot = lax.axis_index("tm"), lax.axis_index("grp")
    where = jnp.stack([me, slot]).astype(jnp.int32)
    channels = features.shape[1]
    taps, groups, width = pos_weight.shape[0], pos_weight.shape[1], pos_weight.shape[2]
    columns = groups * width
    half = taps // 2
    own = features.shape[0] // 4
    block = own * slots

    w_taps = in_hbm(jnp.transpose(pos_weight, (1, 2, 3, 0)))
    blocks = [features] + [swap(features, "grp", e) for e in range(1, slots)]
    bias = pos_bias.reshape(1, columns)
    proj_half = lax.dynamic_slice_in_dim(projection, slot * columns, columns, 1)
    proj_half = jnp.pad(proj_half, ((0, 0), (0, channels - columns)))
    five, offs = spread_near(jnp.transpose(weight_five, (0, 2, 1)), members)
    six, _ = spread_near(jnp.transpose(weight_six, (0, 2, 1)), members)
    last, last_offs = spread_doubling(proj_half[None], members)
    five, layout = spread_far(five, offs, members)
    six, _ = spread_far(six, offs, members)
    last, last_layout = spread_far(last, last_offs, members)
    common = dict(layout=layout)
    taps_scratch = [pltpu.VMEM((2, channels, channels), BF16)]

    cut = (groups + 1) // 2
    tap_sems = lambda count: pltpu.SemaphoreType.DMA((count, 5))
    act_five, w_low = pl.pallas_call(
        functools.partial(five_body, count=slots, **common),
        in_specs=[SMEM_SPEC, HBM_SPEC] + vmem_specs(slots - 1 + len(five)) + [HBM_SPEC],
        out_specs=vmem_specs(2),
        out_shape=[
            pltpu.VMEM((2 * block, channels), BF16),
            pltpu.VMEM((cut, width, width, taps), BF16),
        ],
        scratch_shapes=taps_scratch
        + [tap_sems(cut), pltpu.VMEM(features.shape, BF16), pltpu.SemaphoreType.DMA(())],
        compiler_params=PARAMS,
        name="five",
    )(where, in_hbm(blocks[0]), *on_chip(blocks[1:] + five), w_taps)
    rest = groups - cut
    results = pl.pallas_call(
        functools.partial(six_body, count=slots, start=cut if rest else None, **common),
        in_specs=[SMEM_SPEC] + vmem_specs(1 + len(six)) + ([HBM_SPEC] if rest else []),
        out_specs=vmem_specs(4 if rest else 3),
        out_shape=[
            pltpu.VMEM((block, channels), BF16),
            pltpu.VMEM((own, channels), F32),
            pltpu.VMEM((own, 128), F32),
        ]
        + ([pltpu.VMEM((rest, width, width, taps), BF16)] if rest else []),
        scratch_shapes=taps_scratch + ([tap_sems(rest)] if rest else []),
        compiler_params=PARAMS,
        name="six",
    )(where, act_five, *on_chip(six), *([w_taps] if rest else []))
    normed, unit, inv_dev = results[:3]
    weights = [w_low] + list(results[3:])

    whole = block == half
    tail = normed if whole else normed[block - half :]
    head = normed if whole else normed[:half]
    got_a, got_b = halo(tail, head, me % 2)
    conv_scratch = [
        pltpu.VMEM((columns, taps), F32),
        pltpu.VMEM((columns, taps), F32),
        pltpu.VMEM((groups, half, width), F32),
    ]
    encoded, slope_rev, proj = pl.pallas_call(
        functools.partial(forward_body, held=len(weights), layout=last_layout),
        in_specs=[SMEM_SPEC] + vmem_specs(3 + len(last) + len(weights) + 2),
        out_specs=vmem_specs(3),
        out_shape=[
            jax.ShapeDtypeStruct((block, columns), BF16),
            pltpu.VMEM((block, columns), BF16),
            pltpu.VMEM((channels, columns), BF16),
        ],
        scratch_shapes=[pltpu.VMEM((1, channels, channels), BF16)] + conv_scratch,
        compiler_params=CONV_PARAMS,
        name="forward",
    )(where, normed, *on_chip([got_a, got_b] + last), *weights, cotangent, bias)

    tail = slope_rev if whole else slope_rev[block - half :]
    head = slope_rev if whole else slope_rev[:half]
    got_a, got_b = halo(tail, head, me % 2)
    scale = 1.0 / math.sqrt(own * members * slots)
    share = channels // members
    finals = [0, members // 4, members // 2, 3 * (members // 4)]
    masks, mask = [], 2
    while mask < members // 4:
        masks.append(mask)
        mask *= 2
    order = finals
    for mask in reversed(masks):
        order = order + [p ^ mask for p in order]
    kept, sent, unit_grad, unit_sent = pl.pallas_call(
        functools.partial(backward_body, scale=scale, order=order, held=len(weights)),
        in_specs=[SMEM_SPEC] + vmem_specs(6 + len(weights)),
        out_specs=vmem_specs(4),
        out_shape=[pltpu.VMEM((members // 2, share, columns), BF16)] * 2
        + [
            pltpu.VMEM((own, channels), F32),
            pltpu.VMEM((slots - 1, own, channels), BF16),
        ],
        scratch_shapes=conv_scratch
        + [
            pltpu.VMEM((width, width, taps), BF16),
            pltpu.VMEM((block, columns), BF16),
            pltpu.VMEM((members, share, columns), F32),
            pltpu.VMEM((slots, own, channels), F32),
        ],
        compiler_params=CONV_PARAMS,
        name="backward",
    )(where, slope_rev, *on_chip([got_a, got_b]), *weights, cotangent, normed, proj)

    got = swap(sent, "tm", 1)
    total = (kept.astype(F32) + got.astype(F32)).astype(BF16)
    for mask in masks:
        middle = total.shape[0] // 2
        got = swap(total[middle:], "tm", mask)
        total = (total[:middle].astype(F32) + got.astype(F32)).astype(BF16)
    parts = []
    for n in (1, 2, 3):
        parts.append(swap(total[n], "tm", finals[n]))
    projection_grad = total[0].astype(F32) + sum(p.astype(F32) for p in parts)

    grad_unit = unit_grad
    for e in range(1, slots):
        got = swap(unit_sent[e - 1], "grp", e)
        grad_unit = grad_unit + got.astype(F32)
    first_mean = jnp.mean(grad_unit, axis=-1, keepdims=True)
    second_mean = jnp.mean(grad_unit * unit, axis=-1, keepdims=True)
    feature_grad = (inv_dev[:, :1] * (grad_unit - first_mean - unit * second_mean)).astype(BF16)
    return (encoded, feature_grad, projection_grad)


def solution(mesh):
    in_specs = (
        P(("tm", "grp"), None),
        P(None, None, "tm"),
        P(None, None, "tm"),
        P("tm", None),
        P(None, "grp", None, None),
        P("grp"),
        P("tm", "grp"),
    )
    out_specs = (P("tm", "grp"), P(("tm", "grp"), None), P("tm", "grp"))

    return jax.shard_map(
        on_device, mesh=mesh, in_specs=in_specs, out_specs=out_specs, check_vma=False
    )
```
